512 devices in a mesh: dom: 32 (over x_lo, z), grid: 16 (over x_hi, y, core).
Axes of the slice: x: 4 (x_hi: 2, x_lo: 2; x = x_hi * 2 + x_lo), y: 4, z: 16, core: 2. Of those that a mesh axis runs over, the one named last changes fastest.
Arguments:
- node_feats: bfloat16 [65536, 512], P(('dom', 'grid')), may hold values from -6 to 6
- adj_vals: bfloat16 [32, 16, 16, 4, 128, 128], P('dom', 'grid'), may hold values from -0.109375 to 0.109375
- adj_col: int32 [32, 16, 16, 4], P('dom', 'grid'), may hold values from 0 to 31
- adj_count: int32 [32, 16, 16], P('dom', 'grid'), may hold values from 0 to 4, as said below
- hist_store: bfloat16 [512, 16384], P('grid', 'dom'), may hold values from -6 to 6
- hist_list: int32 [32, 40], replicated, may hold values from 0 to 127, as said below
- hist_adj: bfloat16 [32, 40, 128, 128], P('dom'), may hold values from -0.3125 to 0.3125
- hist_row: int32 [32, 40], P('dom'), may hold values from 0 to 15
- hist_col: int32 [32, 40], P('dom'), may hold values from 0 to 39, each once within a row
- w_first: bfloat16 [512, 512], replicated, may hold values from -0.25 to 0.25
- w_second: bfloat16 [512, 512], replicated, may hold values from -0.25 to 0.25
Outputs:
- hidden: bfloat16 [65536, 512], P(('dom', 'grid'))
- embedding: bfloat16 [65536, 512], P(('dom', 'grid'))
The draws below stay inside these ranges and needn't reach their ends.
Inputs may be any that keep to these rules, and one draw needn't show every extreme that they name: `adj_count`: slots of a block row at or beyond its count hold values that take no part. Some block row of some tile has 4 live slots. `hist_list`: the ids in one partition's list are distinct; at most 2 of them belong to one owner partition (owner = id // 4), and some list has 2 from one owner.
All inputs are finite; a program needn't handle non-finite values.
Results may differ from the reference program's by a relative error of at most 0.024.
Values may be sent and summed in bfloat16 or wider, within the bound.
No kernel may reach another device: no remote copies, remote signals or barrier semaphores. Data moves between devices by JAX's collectives and lax.ppermute only.
A program may use at most 64 MiB of HBM per device.

```python
import jax
import jax.numpy as jnp
from jax import lax

F = 512
BLOCK = 128
BPD = 1
K_MAX = 4
HOWN = 4
LIST = 40
TROWS = 16
TCOLS = 32
NODES = 65536
HIST = 16384
N_DOM = 32
N_GRID = 16


def draw_adj_count(key, part):
    rows_tile = N_GRID * BPD
    first_key, second_key, third_key = jax.random.split(key, 3)
    density = jax.random.randint(first_key, (N_DOM, N_GRID, 1), 1, K_MAX + 1)
    counts = jax.random.randint(second_key, (N_DOM, N_GRID, rows_tile), 0, K_MAX + 1)
    counts = jnp.minimum(counts, density).reshape(-1)
    chosen = jax.random.randint(third_key, (), 0, N_DOM * N_GRID * rows_tile)
    counts = jnp.where(jnp.arange(counts.shape[0]) == chosen, K_MAX, counts)
    return counts.reshape(N_DOM, N_GRID, rows_tile).astype(jnp.int32)


def one_owner_order(owner_key):
    return jax.random.permutation(owner_key, HOWN)


def one_reader(reader_key):
    twos = N_DOM * 3 // 8
    singles = N_DOM // 2
    first_key, second_key, third_key = jax.random.split(reader_key, 3)
    owners = jax.random.permutation(first_key, N_DOM)
    inner_order = jax.vmap(one_owner_order)(jax.random.split(second_key, N_DOM))
    first_ids = owners[:twos] * HOWN + inner_order[:twos, 0]
    second_ids = owners[:twos] * HOWN + inner_order[:twos, 1]
    single_ids = owners[twos:twos + singles] * HOWN + inner_order[twos:twos + singles, 0]
    all_ids = jnp.concatenate([first_ids, second_ids, single_ids])
    return jax.random.permutation(third_key, all_ids)


def draw_hist_list(key, part):
    reader_keys = jax.random.split(key, N_DOM)
    return jax.vmap(one_reader)(reader_keys).astype(jnp.int32)


def set_ends(values, own_key, smallest, top_value):
    place = [jax.random.randint(jax.random.fold_in(own_key, axis), (), 0, length) for axis, length in enumerate(values.shape)]
    main_axis = values.shape.index(max(values.shape))
    beside = place[:main_axis] + [(place[main_axis] + 1) % values.shape[main_axis]] + place[main_axis + 1:]
    return values.at[tuple(place)].set(smallest).at[tuple(beside)].set(top_value)


def block_levels(key, dims, pieces, low, high):
    gain, own = 1.0, jax.random.fold_in(key, 6)
    for dim, shards_of in pieces:
        draws = jnp.exp(jax.random.uniform(jax.random.fold_in(own, dim), (shards_of,), jnp.float32, low / len(pieces), high / len(pieces)))
        gain = gain * jnp.repeat(draws, dims[dim] // shards_of).reshape([-1 if axis == dim else 1 for axis in range(len(dims))])
    return gain


def scatter_about(rng, extent, width, bound, pieces=(), kind=jnp.bfloat16):
    loudness = block_levels(rng, extent, pieces, -0.22, 0.18) if pieces else 1.0
    array = jax.random.normal(rng, extent, jnp.float32) * width * loudness
    return jnp.minimum(jnp.maximum(array, -bound), bound).astype(kind)


def setup_inputs(seed: int = 0) -> dict:
    key_of = jax.random.split(jax.random.key(seed), 12)
    node_feats = scatter_about(key_of[0], (NODES, F), 1.0, 6.0, ((0, 512),))
    adj_vals = scatter_about(key_of[1], (N_DOM, N_GRID, TROWS, K_MAX, BLOCK, BLOCK), (BLOCK * K_MAX * N_GRID // 3) ** -0.5, 0.109375, ((0, 32), (1, 16)))
    adj_col = set_ends(jax.random.randint(key_of[2], (N_DOM, N_GRID, TROWS, K_MAX), 0, TCOLS), jax.random.fold_in(key_of[2], 1), 0, TCOLS - 1).astype(jnp.int32)
    adj_count = draw_adj_count(jax.random.fold_in(key_of[11], 71), 0)
    hist_store = scatter_about(key_of[4], (F, HIST), 1.0, 6.0, ((0, 16), (1, 32)))
    hist_list = draw_hist_list(jax.random.fold_in(key_of[11], 71), 0)
    hist_adj = scatter_about(key_of[6], (N_DOM, LIST, BLOCK, BLOCK), (BLOCK * LIST // (N_GRID * BPD)) ** -0.5, 0.3125, ((0, 32),))
    hist_row = set_ends(jax.random.randint(key_of[7], (N_DOM, LIST), 0, TROWS), jax.random.fold_in(key_of[7], 1), 0, TROWS - 1).astype(jnp.int32)
    hist_col = jax.vmap(lambda own: jax.random.permutation(own, LIST))(jax.random.split(key_of[8], N_DOM)).reshape((N_DOM, LIST)).astype(jnp.int32)
    w_first = scatter_about(key_of[9], (F, F), F ** -0.5, 0.25)
    w_second = scatter_about(key_of[10], (F, F), F ** -0.5, 0.25)
    return {"node_feats": node_feats, "adj_vals": adj_vals, "adj_col": adj_col, "adj_count": adj_count, "hist_store": hist_store, "hist_list": hist_list, "hist_adj": hist_adj, "hist_row": hist_row, "hist_col": hist_col, "w_first": w_first, "w_second": w_second}


def no_history(row_index):
    return jnp.zeros((), jnp.float32)


def tile_sums(source, adj_vals, adj_col, adj_count, extra_fn):
    rows_tile = N_GRID * BPD
    cols_tile = N_DOM * BPD
    feat_cols = F // N_GRID
    grid_view = source.reshape(N_DOM, N_GRID, BPD * BLOCK, F)
    column_group = (jnp.arange(F) // feat_cols).astype(jnp.int32)

    def one_partition(row_index):
        extra_term = extra_fn(row_index)

        def one_tile(running, col_index):
            col_panel = lax.dynamic_index_in_dim(grid_view, col_index, 1, keepdims=False)
            col_blocks = col_panel.reshape(cols_tile, BLOCK, F).astype(jnp.float32)
            picked = col_blocks[adj_col[row_index, col_index]]
            live_mask = (jnp.arange(K_MAX)[None, :] < adj_count[row_index, col_index][:, None]).astype(jnp.float32)
            weights = adj_vals[row_index, col_index].astype(jnp.float32) * live_mask[:, :, None, None]
            summed = jnp.einsum("rkab,rkbf->raf", weights, picked).reshape(rows_tile * BLOCK, F)
            summed = summed + jnp.where((column_group == col_index)[None, :], extra_term, 0.0)
            rounded = lax.optimization_barrier(summed.astype(jnp.bfloat16))
            return running + rounded.astype(jnp.float32), None

        start = jnp.zeros((rows_tile * BLOCK, F), jnp.float32)
        running, unused = lax.scan(one_tile, start, jnp.arange(N_GRID).astype(jnp.int32))
        return running.astype(jnp.bfloat16)

    result = lax.map(one_partition, jnp.arange(N_DOM).astype(jnp.int32))
    return result.reshape(N_DOM * rows_tile * BLOCK, F)


def reference(node_feats, adj_vals, adj_col, adj_count, hist_store, hist_list, hist_adj, hist_row, hist_col, w_first, w_second):
    store_blocks = hist_store.T.reshape(N_DOM * HOWN, BLOCK, F).astype(jnp.float32)

    def history_rows(row_index):
        fetched = store_blocks[hist_list[row_index]]
        chosen = fetched[hist_col[row_index]]
        contribs = jnp.einsum("sab,sbf->saf", hist_adj[row_index].astype(jnp.float32), chosen)
        row_onehot = (hist_row[row_index][None, :] == jnp.arange(N_GRID * BPD)[:, None]).astype(jnp.float32)
        summed = jnp.einsum("rs,saf->raf", row_onehot, contribs, precision=lax.Precision.HIGHEST)
        return summed.reshape(N_GRID * BPD * BLOCK, F)

    agg_first = tile_sums(node_feats, adj_vals, adj_col, adj_count, no_history)
    hidden = jax.nn.relu(jnp.dot(agg_first, w_first, preferred_element_type=jnp.float32)).astype(jnp.bfloat16)
    agg_second = tile_sums(hidden, adj_vals, adj_col, adj_count, history_rows)
    embedding = jnp.dot(agg_second, w_second, preferred_element_type=jnp.float32).astype(jnp.bfloat16)
    return hidden, embedding
```

```python
import functools

import jax
import jax.numpy as jnp
from jax import lax
from jax.experimental import pallas as pl
from jax.experimental.pallas import tpu as pltpu
from jax.sharding import Mesh, PartitionSpec as P

F = 512
BLOCK = 128
HOWN = 4
ROWS = 16
SLOTS = 4
FEAT = 32
LIST = 40
WIDE = 128
STRIDE = BLOCK + FEAT
DOM = ("x_lo", "z")
GRID = ("x_hi", "y", "core")
SIDE = ("x_hi", "y")


def tile_body(stride, cols, counts, spot, adj, panel, *rest):
    extra = rest[0] if len(rest) == 4 else None
    keep, send, acc = rest[-3:]
    row = pl.program_id(0)
    count = counts[row]
    core = spot[0]

    def pair(first):
        left = []
        right = []
        for slot in (first, first + 1):
            live = slot < count
            left.append(jnp.where(live, adj[0, slot], jnp.zeros_like(adj[0, slot])))
            start = pl.multiple_of(cols[row * SLOTS + slot] * stride, FEAT)
            right.append(panel[pl.ds(start, BLOCK), :])
        return jnp.dot(
            jnp.concatenate(left, axis=1),
            jnp.concatenate(right, axis=0),
            preferred_element_type=jnp.float32,
        )

    acc[...] = pair(0)

    @pl.when(count > 2)
    def _():
        acc[...] += pair(2)

    if extra is not None:
        for lane in range(F // WIDE):

            @pl.when(spot[1] == lane)
            def _(lane=lane):
                acc[:, lane * WIDE : (lane + 1) * WIDE] += extra[...]

    value = acc[...].astype(jnp.bfloat16)

    @pl.when(row % 2 == core)
    def _():
        keep[0] = value

    @pl.when(row % 2 != core)
    def _():
        send[0] = value


def tile_product(cols, counts, spot, adj, panel, extra):
    operands = [adj, panel]
    specs = [
        pl.BlockSpec((1, SLOTS, BLOCK, BLOCK), lambda q, *_: (q, 0, 0, 0)),
        pl.BlockSpec(panel.shape, lambda q, *_: (0, 0)),
    ]
    if extra is not None:
        operands.append(extra)
        specs.append(pl.BlockSpec((BLOCK, WIDE), lambda q, *_: (q, 0)))
    half = jax.ShapeDtypeStruct((ROWS // 2, BLOCK, F), jnp.bfloat16)
    out_spec = pl.BlockSpec((1, BLOCK, F), lambda q, *_: (q // 2, 0, 0))
    return pl.pallas_call(
        functools.partial(tile_body, panel.shape[0] // 32),
        out_shape=(half, half),
        grid_spec=pltpu.PrefetchScalarGridSpec(
            num_scalar_prefetch=3,
            grid=(ROWS,),
            in_specs=specs,
            out_specs=(out_spec, out_spec),
            scratch_shapes=[pltpu.VMEM((BLOCK, F), jnp.float32)],
        ),
        compiler_params=pltpu.CompilerParams(
            dimension_semantics=("arbitrary",), vmem_limit_bytes=40 << 20
        ),
        name="tile_product",
    )(cols, counts, spot, *operands)


def history_body(places, rows, spot, adj, store, out, wide):
    wide[...] = jnp.zeros_like(wide)
    out[...] = jnp.zeros_like(out)
    offset = pl.multiple_of(spot[2] * FEAT, FEAT)

    def step(slot, carry):
        source = pl.multiple_of((places[slot] // HOWN) * STRIDE + BLOCK, FEAT)
        lane = pl.multiple_of((places[slot] % HOWN) * BLOCK, BLOCK)
        wide[pl.ds(offset, FEAT), :] = store[pl.ds(source, FEAT), pl.ds(lane, BLOCK)]
        part = lax.dot_general(
            adj[slot], wide[...], (((1,), (1,)), ((), ())), preferred_element_type=jnp.float32
        )
        target = pl.multiple_of(rows[slot] * BLOCK, BLOCK)
        out[pl.ds(target, BLOCK), :] += part
        return carry

    lax.fori_loop(0, LIST, step, 0)


def history_term(places, rows, spot, adj, store):
    return pl.pallas_call(
        history_body,
        out_shape=jax.ShapeDtypeStruct((ROWS * BLOCK, WIDE), jnp.float32),
        grid_spec=pltpu.PrefetchScalarGridSpec(
            num_scalar_prefetch=3,
            grid=(1,),
            in_specs=[
                pl.BlockSpec(adj.shape, lambda i, *_: (0, 0, 0)),
                pl.BlockSpec(store.shape, lambda i, *_: (0, 0)),
            ],
            out_specs=pl.BlockSpec((ROWS * BLOCK, WIDE), lambda i, *_: (0, 0)),
            scratch_shapes=[pltpu.VMEM((WIDE, BLOCK), jnp.bfloat16)],
        ),
        compiler_params=pltpu.CompilerParams(
            dimension_semantics=("arbitrary",), vmem_limit_bytes=40 << 20
        ),
        name="history_term",
    )(places, rows, spot, adj, store)


def finish(parts, weight, relu):
    def body(parts_ref, weight_ref, out):
        total = parts_ref[0].astype(jnp.float32)
        for k in range(1, parts.shape[0]):
            total = total + parts_ref[k].astype(jnp.float32)
        value = jnp.dot(
            total.astype(jnp.bfloat16), weight_ref[...], preferred_element_type=jnp.float32
        )
        if relu:
            value = jnp.maximum(value, 0.0)
        out[...] = value.astype(jnp.bfloat16)

    return pl.pallas_call(
        body,
        out_shape=jax.ShapeDtypeStruct((BLOCK, F), jnp.bfloat16),
        compiler_params=pltpu.CompilerParams(vmem_limit_bytes=32 << 20),
        name="finish",
    )(parts, weight)


def gather_panel(source):
    pair = lax.all_gather(source, "x_lo", axis=0, tiled=True)
    return lax.all_gather(pair, "z", axis=0, tiled=True)


def reduce_rows(keep, send):
    swap = [(0, 1), (1, 0)]
    other = lax.ppermute(send, "core", swap)
    both = (keep.astype(jnp.float32) + other.astype(jnp.float32)).astype(jnp.bfloat16)
    return lax.all_to_all(both, SIDE, 0, 0, tiled=True)


def local(
    node_feats,
    adj_vals,
    adj_col,
    adj_count,
    hist_store,
    hist_list,
    hist_adj,
    hist_row,
    hist_col,
    w_first,
    w_second,
):
    adj = adj_vals[0, 0]
    cols = adj_col[0, 0].reshape(-1)
    counts = adj_count[0, 0]
    places = (cols % 16) * 2 + cols // 16
    grid_index = lax.axis_index(GRID)
    spot = jnp.stack([lax.axis_index("core"), grid_index // 4, grid_index % 4]).astype(jnp.int32)

    panel = gather_panel(jnp.concatenate([node_feats, hist_store], axis=0))

    mine = lax.dynamic_index_in_dim(hist_list, lax.axis_index(DOM), 0, keepdims=False)
    wanted = jnp.take(mine, hist_col[0], axis=0)
    owner = wanted // HOWN
    hist_places = ((owner % 16) * 2 + owner // 16) * HOWN + wanted % HOWN
    extra = history_term(hist_places, hist_row[0], spot, hist_adj[0], panel)

    hidden = finish(
        reduce_rows(*tile_product(places, counts, spot, adj, panel, None)), w_first, True
    )
    panel = gather_panel(hidden)
    embedding = finish(
        reduce_rows(*tile_product(places, counts, spot, adj, panel, extra)), w_second, False
    )
    return hidden, embedding


def solution(mesh):
    fine = Mesh(mesh.devices.reshape(2, 16, 2, 4, 2), ("x_lo", "z", "x_hi", "y", "core"))
    placed = (
        P(DOM + GRID, None),
        P(DOM, GRID),
        P(DOM, GRID),
        P(DOM, GRID),
        P(GRID, DOM),
        P(),
        P(DOM),
        P(DOM),
        P(DOM),
        P(),
        P(),
    )
    return jax.shard_map(
        local,
        mesh=fine,
        in_specs=placed,
        out_specs=(P(DOM + GRID, None), P(DOM + GRID, None)),
        check_vma=False,
    )
```

```python
import functools

import jax
import jax.numpy as jnp
from jax import lax
from jax.experimental import pallas as pl
from jax.experimental.pallas import tpu as pltpu
from jax.sharding import Mesh, PartitionSpec as P

F = 512
HALF = 256
BLOCK = 128
HOWN = 4
ROWS = 16
SLOTS = 4
FEAT = 32
LIST = 40
WIDE = 128
META = 16
PAY = BLOCK + 2 * FEAT + META
DOM = ("x_lo", "zh", "zl")
Z = ("zh", "zl")
GRID = ("x_hi", "y", "core")
SIDE = ("x_hi", "y")
SWAP = [(0, 1), (1, 0)]
UP = [(z, (z + 1) % 16) for z in range(16)]
DOWN = [(z, (z + 15) % 16) for z in range(16)]


def params(mib):
    return pltpu.CompilerParams(vmem_limit_bytes=mib << 20)


def payload_body(feats, hist, meta, out):
    for j in range(2):
        out[j, :BLOCK] = feats[:, j * HALF : (j + 1) * HALF]
        for k in range(2):
            start = BLOCK + k * FEAT
            out[j, start : start + FEAT] = hist[:, k * HALF : (k + 1) * HALF]
        out[j, BLOCK + 2 * FEAT :] = meta[...]


def make_payload(feats, hist, meta):
    return pl.pallas_call(
        payload_body,
        out_shape=jax.ShapeDtypeStruct((2, PAY, HALF), jnp.bfloat16),
        compiler_params=params(8),
        name="payload",
    )(feats, hist, meta)


def tile_body(with_extra, places, counts, spot, own, partner, same, above, below, *rest):
    extras = rest[:2] if with_extra else ()
    keep, send, panel, adj, acc, sems = rest[-6:]
    core = spot[1]
    moves = [
        pltpu.make_async_copy(same, panel.at[pl.ds(0, 2048)], sems.at[0]),
        pltpu.make_async_copy(above, panel.at[pl.ds(2048, 1024)], sems.at[1]),
        pltpu.make_async_copy(below, panel.at[pl.ds(3072, 1024)], sems.at[2]),
    ]
    for k, source in enumerate((own, partner)):
        for c in range(4):
            moves.append(
                pltpu.make_async_copy(
                    source.at[pl.ds(16 * c, 16)],
                    adj.at[pl.ds(64 * k + 16 * c, 16)],
                    sems.at[3 + 4 * k + c],
                )
            )
    for move in moves:
        move.start()

    def pair(base, count, first):
        left = []
        right = []
        for slot in (first, first + 1):
            block = adj[base + slot]
            left.append(jnp.where(slot < count, block, jnp.zeros_like(block)))
            start = pl.multiple_of(places[base + slot] * BLOCK, BLOCK)
            right.append(panel[pl.ds(start, BLOCK), :])
        return jnp.dot(
            jnp.concatenate(left, axis=1),
            jnp.concatenate(right, axis=0),
            preferred_element_type=jnp.float32,
        )

    def two_rows(k, j):
        part = spot[0] if k == 0 else 1 - spot[0]
        for side in range(2):
            row = 2 * j + side
            count = counts[ROWS * k + row]
            base = (ROWS * k + row) * SLOTS
            acc[side] = pair(base, count, 0)

            @pl.when(count > 2)
            def _(side=side, base=base, count=count):
                acc[side] += pair(base, count, 2)

            if with_extra:
                for group in range(2):

                    @pl.when(spot[2] == group)
                    def _(side=side, group=group, row=row):
                        start = pl.multiple_of(row * BLOCK, BLOCK)
                        piece = extras[k][pl.ds(start, BLOCK), :].astype(jnp.float32)
                        acc[side, :, group * WIDE : (group + 1) * WIDE] += piece

        even = acc[0].astype(jnp.bfloat16)
        odd = acc[1].astype(jnp.bfloat16)
        keep[j, part] = jnp.where(core == 0, even, odd)
        send[j, part] = jnp.where(core == 0, odd, even)

    for n in range(3):
        moves[n].wait()
    for k in range(2):
        for c in range(4):
            moves[3 + 4 * k + c].wait()

            def step(j, carry, k=k):
                two_rows(k, j)
                return carry

            lax.fori_loop(2 * c, 2 * c + 2, step, 0)


def tile_product(places, counts, spot, own, partner, panels, extras):
    operands = [own, partner, *panels]
    specs = [pl.BlockSpec(memory_space=pl.ANY)] * 5
    for extra in extras:
        operands.append(extra)
        specs.append(pl.BlockSpec(extra.shape, lambda i, *_: (0, 0)))
    half = jax.ShapeDtypeStruct((ROWS // 2, 2, BLOCK, HALF), jnp.bfloat16)
    out_spec = pl.BlockSpec(half.shape, lambda i, *_: (0, 0, 0, 0))
    return pl.pallas_call(
        functools.partial(tile_body, bool(extras)),
        out_shape=(half, half),
        grid_spec=pltpu.PrefetchScalarGridSpec(
            num_scalar_prefetch=3,
            grid=(1,),
            in_specs=specs,
            out_specs=(out_spec, out_spec),
            scratch_shapes=[
                pltpu.VMEM((4096, HALF), jnp.bfloat16),
                pltpu.VMEM((2 * ROWS * SLOTS, BLOCK, BLOCK), jnp.bfloat16),
                pltpu.VMEM((2, BLOCK, HALF), jnp.float32),
                pltpu.SemaphoreType.DMA((11,)),
            ],
        ),
        compiler_params=params(20),
        name="tile_product",
    )(places, counts, spot, *operands)


def history_body(listed, order, rows, spot, adj, store, out, total, wide):
    wide[...] = jnp.zeros_like(wide)
    total[...] = jnp.zeros_like(total)
    offset = pl.multiple_of(spot[1] * FEAT, FEAT)

    def step(slot, carry):
        block = listed[spot[0], order[slot]]
        owner = block // HOWN
        piece = block % HOWN
        spot_row = ((owner % 16) * 2 + owner // 16) * (2 * FEAT) + (piece // 2) * FEAT
        source = pl.multiple_of(spot_row, FEAT)
        lane = pl.multiple_of((piece % 2) * BLOCK, BLOCK)
        wide[pl.ds(offset, FEAT), :] = store[pl.ds(source, FEAT), pl.ds(lane, BLOCK)]
        part = lax.dot_general(
            adj[slot], wide[...], (((1,), (1,)), ((), ())), preferred_element_type=jnp.float32
        )
        target = pl.multiple_of(rows[slot] * BLOCK, BLOCK)
        total[pl.ds(target, BLOCK), :] += part
        return carry

    lax.fori_loop(0, LIST, step, 0)
    out[...] = total[...].astype(jnp.bfloat16)


def history_term(listed, order, rows, spot, adj, store):
    return pl.pallas_call(
        history_body,
        out_shape=jax.ShapeDtypeStruct((ROWS * BLOCK, WIDE), jnp.bfloat16),
        grid_spec=pltpu.PrefetchScalarGridSpec(
            num_scalar_prefetch=4,
            grid=(1,),
            in_specs=[
                pl.BlockSpec(adj.shape, lambda i, *_: (0, 0, 0)),
                pl.BlockSpec(store.shape, lambda i, *_: (0, 0)),
            ],
            out_specs=pl.BlockSpec((ROWS * BLOCK, WIDE), lambda i, *_: (0, 0)),
            scratch_shapes=[
                pltpu.VMEM((ROWS * BLOCK, WIDE), jnp.float32),
                pltpu.VMEM((WIDE, BLOCK), jnp.bfloat16),
            ],
        ),
        compiler_params=params(16),
        name="history_term",
    )(listed, order, rows, spot, adj, store)


def add_parts(parts):
    def body(parts_ref, out):
        total = parts_ref[0].astype(jnp.float32)
        for k in range(1, parts.shape[0]):
            total = total + parts_ref[k].astype(jnp.float32)
        out[...] = total.astype(jnp.bfloat16)

    return pl.pallas_call(
        body,
        out_shape=jax.ShapeDtypeStruct(parts.shape[1:], jnp.bfloat16),
        compiler_params=params(8),
        name="add_parts",
    )(parts)


def first_dense(halves, weight, spot):
    def body(spot_ref, halves_ref, weight_ref, hidden, chunk):
        rows = [
            jnp.concatenate([halves_ref[0, part], halves_ref[1, part]], axis=1)
            for part in range(2)
        ]
        value = jnp.dot(
            jnp.concatenate(rows, axis=0), weight_ref[...], preferred_element_type=jnp.float32
        )
        value = jnp.maximum(value, 0.0).astype(jnp.bfloat16)
        low = spot_ref[0] == 0
        hidden[...] = jnp.where(low, value[:BLOCK], value[BLOCK:])
        chunk[...] = jnp.where(low, value[:, :HALF], value[:, HALF:])

    return pl.pallas_call(
        body,
        out_shape=(
            jax.ShapeDtypeStruct((BLOCK, F), jnp.bfloat16),
            jax.ShapeDtypeStruct((2 * BLOCK, HALF), jnp.bfloat16),
        ),
        grid_spec=pltpu.PrefetchScalarGridSpec(
            num_scalar_prefetch=1,
            grid=(1,),
            in_specs=[
                pl.BlockSpec(halves.shape, lambda i, *_: (0, 0, 0, 0)),
                pl.BlockSpec(weight.shape, lambda i, *_: (0, 0)),
            ],
            out_specs=(
                pl.BlockSpec((BLOCK, F), lambda i, *_: (0, 0)),
                pl.BlockSpec((2 * BLOCK, HALF), lambda i, *_: (0, 0)),
            ),
        ),
        compiler_params=params(8),
        name="first_dense",
    )(spot, halves, weight)


def second_dense(halves, weight):
    def body(halves_ref, weight_ref, out):
        rows = jnp.concatenate([halves_ref[0], halves_ref[1]], axis=1)
        value = jnp.dot(rows, weight_ref[...], preferred_element_type=jnp.float32)
        out[...] = value.astype(jnp.bfloat16)

    return pl.pallas_call(
        body,
        out_shape=jax.ShapeDtypeStruct((BLOCK, F), jnp.bfloat16),
        compiler_params=params(8),
        name="second_dense",
    )(halves, weight)


def gather_panel(chunk, first=None):
    same = lax.all_gather(chunk, "zh", axis=0, tiled=True)
    if first is not None:
        same, first = lax.optimization_barrier((same, first))
    above = lax.ppermute(same[:1024], Z, DOWN)
    below = lax.ppermute(same[1024:], Z, UP)
    panels = (same, above, below)
    return panels if first is None else (panels, first)


def reduce_rows(keep, send):
    other = lax.ppermute(send, "core", SWAP)
    both = (keep.astype(jnp.float32) + other.astype(jnp.float32)).astype(jnp.bfloat16)
    return add_parts(lax.all_to_all(both, SIDE, 0, 0, tiled=True))


def local(
    node_feats,
    adj_vals,
    adj_col,
    adj_count,
    hist_store,
    hist_list,
    hist_adj,
    hist_row,
    hist_col,
    w_first,
    w_second,
):
    adj = adj_vals[0, 0].reshape(ROWS * SLOTS, BLOCK, BLOCK)
    x_lo = lax.axis_index("x_lo")
    x_hi = lax.axis_index("x_hi")
    zl = lax.axis_index("zl")
    grid_index = lax.axis_index(GRID)
    group = jnp.where(x_lo == x_hi, (grid_index // 4) % 2, -1)
    spot = jnp.stack([x_lo, lax.axis_index("core"), group]).astype(jnp.int32)
    hist_spot = jnp.stack([lax.axis_index(DOM), grid_index % 4]).astype(jnp.int32)

    numbers = jnp.concatenate([adj_col.reshape(-1), adj_count.reshape(-1)])
    meta = jnp.pad(numbers.astype(jnp.bfloat16)[None, :], ((0, META - 1), (0, HALF - 80)))
    payload = make_payload(node_feats, hist_store, meta)
    received = lax.all_to_all(payload, "x_lo", 0, 0, tiled=True)
    adj_held, received = lax.optimization_barrier((adj, received))
    near = lax.all_gather(
        received[:, BLOCK : BLOCK + 2 * FEAT].reshape(4 * FEAT, HALF), "zl", axis=0, tiled=True
    )
    panels, near = gather_panel(received[:, :BLOCK].reshape(2 * BLOCK, HALF), near)
    partner = lax.ppermute(adj_held, "x_lo", SWAP)

    theirs = lax.dynamic_index_in_dim(received[:, BLOCK + 2 * FEAT, :80], 1 - x_lo, 0, False)
    both = jnp.stack([numbers, theirs.astype(jnp.int32)])
    cols = both[:, :64]
    places = ((cols & 1) ^ zl) * 16 + ((cols & 15) >> 1) * 2 + (cols >> 4)
    places = places.reshape(-1).astype(jnp.int32)
    counts = both[:, 64:].reshape(-1)

    store = lax.all_gather(near, "zh", axis=0, tiled=True)
    mine = history_term(hist_list, hist_col[0], hist_row[0], hist_spot, hist_adj[0], store)
    extras = (mine, lax.ppermute(mine, "x_lo", SWAP))

    agg = reduce_rows(*tile_product(places, counts, spot, adj, partner, panels, ()))
    halves = lax.all_gather(agg, "x_lo", axis=0, tiled=False)
    hidden, chunk = first_dense(halves, w_first, spot)

    panels = gather_panel(chunk)
    agg = reduce_rows(*tile_product(places, counts, spot, adj, partner, panels, extras))
    embedding = second_dense(lax.all_to_all(agg, "x_lo", 0, 0, tiled=True), w_second)
    return hidden, embedding


def solution(mesh):
    fine = Mesh(
        mesh.devices.reshape(2, 8, 2, 2, 4, 2), ("x_lo", "zh", "zl", "x_hi", "y", "core")
    )
    placed = (
        P(DOM + GRID, None),
        P(DOM, GRID),
        P(DOM, GRID),
        P(DOM, GRID),
        P(GRID, DOM),
        P(),
        P(DOM),
        P(DOM),
        P(DOM),
        P(),
        P(),
    )
    return jax.shard_map(
        local,
        mesh=fine,
        in_specs=placed,
        out_specs=(P(DOM + GRID, None), P(DOM + GRID, None)),
        check_vma=False,
    )
```

```python
import functools

import jax
import jax.numpy as jnp
from jax import lax
from jax.experimental import pallas as pl
from jax.experimental.pallas import tpu as pltpu
from jax.sharding import Mesh, PartitionSpec as P

F = 512
HALF = 256
BLOCK = 128
HOWN = 4
ROWS = 16
SLOTS = 4
FEAT = 32
LIST = 40
WIDE = 128
META = 16
CARRY = BLOCK + 2 * FEAT
PAY = CARRY + META
DOM = ("x_lo", "z")
GRID = ("x_hi", "y", "core")
SIDE = ("x_hi", "y")
SWAP = [(0, 1), (1, 0)]
UP = [(z, (z + 1) % 16) for z in range(16)]
DOWN = [(z, (z + 15) % 16) for z in range(16)]


def params(mib):
    return pltpu.CompilerParams(vmem_limit_bytes=mib << 20)


def payload_body(cols, counts, feats, hist, out, feats_in, hist_in, sems):
    moves = [
        pltpu.make_async_copy(feats, feats_in, sems.at[0]),
        pltpu.make_async_copy(hist, hist_in, sems.at[1]),
    ]
    for move in moves:
        move.start()
    lane = lax.broadcasted_iota(jnp.int32, (META, HALF), 1)
    meta = jnp.zeros((META, HALF), jnp.float32)
    for row in range(ROWS):
        for slot in range(SLOTS):
            meta = jnp.where(lane == row * SLOTS + slot, cols[slot, row].astype(jnp.float32), meta)
        meta = jnp.where(lane == ROWS * SLOTS + row, counts[row].astype(jnp.float32), meta)
    meta = meta.astype(jnp.bfloat16)
    for move in moves:
        move.wait()
    for j in range(2):
        out[j, :BLOCK] = feats_in[:, j * HALF : (j + 1) * HALF]
        for k in range(2):
            start = BLOCK + k * FEAT
            out[j, start : start + FEAT] = hist_in[:, k * HALF : (k + 1) * HALF]
        out[j, CARRY:] = meta


def make_payload(cols, counts, feats, hist):
    return pl.pallas_call(
        payload_body,
        out_shape=jax.ShapeDtypeStruct((2, PAY, HALF), jnp.bfloat16),
        grid_spec=pltpu.PrefetchScalarGridSpec(
            num_scalar_prefetch=2,
            grid=(1,),
            in_specs=[pl.BlockSpec(memory_space=pltpu.HBM)] * 2,
            out_specs=pl.BlockSpec((2, PAY, HALF), lambda i, *_: (0, 0, 0)),
            scratch_shapes=[
                pltpu.VMEM(feats.shape, jnp.bfloat16),
                pltpu.VMEM(hist.shape, jnp.bfloat16),
                pltpu.SemaphoreType.DMA((2,)),
            ],
        ),
        compiler_params=params(8),
        name="payload",
    )(cols, counts, feats, hist)


def tile_body(n_chunks, stride, with_extra, cols, counts, theirs, spot, own, partner, *rest):
    chunks = rest[:n_chunks]
    extras = rest[n_chunks : n_chunks + 2] if with_extra else ()
    keep, send, panel, adj, sems = rest[-5:]
    core = spot[1]
    moves = []
    start = 0
    for source in chunks:
        size = source.shape[0]
        target = panel.at[pl.ds(start, size)]
        moves.append(pltpu.make_async_copy(source, target, sems.at[len(moves)]))
        start += size
    for k, source in enumerate((own, partner)):
        for c in range(4):
            target = adj.at[pl.ds(64 * k + 16 * c, 16)]
            moves.append(
                pltpu.make_async_copy(
                    source.at[pl.ds(16 * c, 16)], target, sems.at[len(moves)]
                )
            )
    for move in moves:
        move.start()

    def product(k, row):
        base = (ROWS * k + row) * SLOTS
        count = counts[row] if k == 0 else theirs[ROWS * SLOTS + row]
        left = []
        right = []
        for slot in range(SLOTS):
            block = adj[base + slot]
            left.append(jnp.where(slot < count, block, jnp.zeros_like(block)))
            col = cols[slot, row] if k == 0 else theirs[row * SLOTS + slot]
            place = (((col & 15) - spot[3]) & 15) * 2 + (col >> 4)
            right.append(panel[pl.ds(pl.multiple_of(place * stride, 2 * FEAT), BLOCK), :])
        return jnp.dot(
            jnp.concatenate(left, axis=1),
            jnp.concatenate(right, axis=0),
            preferred_element_type=jnp.float32,
        )

    def with_history(k, row, value):
        start = pl.multiple_of(row * BLOCK, BLOCK)
        piece = extras[k][pl.ds(start, BLOCK), :].astype(jnp.float32)
        zero = jnp.zeros_like(piece)
        wide = [jnp.where(spot[2] == group, piece, zero) for group in range(2)]
        return value + jnp.concatenate(wide, axis=1)

    def two_rows(k, j):
        part = spot[0] if k == 0 else 1 - spot[0]
        pair = [product(k, 2 * j + side) for side in range(2)]
        if with_extra:
            pair = [with_history(k, 2 * j + side, pair[side]) for side in range(2)]
        even, odd = [value.astype(jnp.bfloat16) for value in pair]
        keep[j, part] = jnp.where(core == 0, even, odd)
        send[j, part] = jnp.where(core == 0, odd, even)

    for n in range(n_chunks):
        moves[n].wait()
    for k in range(2):
        for c in range(4):
            moves[n_chunks + 4 * k + c].wait()
            two_rows(k, 2 * c)
            two_rows(k, 2 * c + 1)


def tile_product(cols, counts, theirs, spot, own, partner, chunks, extras):
    operands = [own, partner, *chunks]
    specs = [pl.BlockSpec(memory_space=pltpu.HBM)] * len(operands)
    stride = chunks[0].shape[0] // 2
    for extra in extras:
        operands.append(extra)
        specs.append(pl.BlockSpec(extra.shape, lambda i, *_: (0, 0)))
    half = jax.ShapeDtypeStruct((ROWS // 2, 2, BLOCK, HALF), jnp.bfloat16)
    out_spec = pl.BlockSpec(half.shape, lambda i, *_: (0, 0, 0, 0))
    return pl.pallas_call(
        functools.partial(tile_body, len(chunks), stride, bool(extras)),
        out_shape=(half, half),
        grid_spec=pltpu.PrefetchScalarGridSpec(
            num_scalar_prefetch=4,
            grid=(1,),
            in_specs=specs,
            out_specs=(out_spec, out_spec),
            scratch_shapes=[
                pltpu.VMEM((32 * stride, HALF), jnp.bfloat16),
                pltpu.VMEM((2 * ROWS * SLOTS, BLOCK, BLOCK), jnp.bfloat16),
                pltpu.SemaphoreType.DMA((len(chunks) + 8,)),
            ],
        ),
        compiler_params=params(20),
        name="tile_product",
    )(cols, counts, theirs, spot, *operands)


def history_body(n_chunks, listed, order, rows, spot, adj, *rest):
    chunks = rest[:n_chunks]
    out, weights, store, total, sems = rest[n_chunks:]
    moves = [pltpu.make_async_copy(adj, weights, sems.at[0])]
    start = 0
    for source in chunks:
        for k in range(source.shape[0] // CARRY):
            moves.append(
                pltpu.make_async_copy(
                    source.at[pl.ds(k * CARRY + BLOCK, 2 * FEAT)],
                    store.at[pl.ds(start, 2 * FEAT)],
                    sems.at[len(moves)],
                )
            )
            start += 2 * FEAT
    for move in moves:
        move.start()
    total[...] = jnp.zeros_like(total)
    for move in moves:
        move.wait()

    def one(slot):
        block = listed[spot[0], order[slot]]
        owner = block >> 2
        piece = block & 3
        place = (((owner & 15) - spot[2]) & 15) * 2 + (owner >> 4)
        source = pl.multiple_of(place * (2 * FEAT) + (piece >> 1) * FEAT, FEAT)
        lane = pl.multiple_of((piece & 1) * BLOCK, BLOCK)
        return lax.dot_general(
            weights[slot],
            store[pl.ds(source, FEAT), pl.ds(lane, BLOCK)],
            (((1,), (1,)), ((), ())),
            preferred_element_type=jnp.float32,
        )

    def step(n, carry):
        parts = [one(n * 5 + k) for k in range(5)]
        for k, part in enumerate(parts):
            target = pl.multiple_of(rows[n * 5 + k] * BLOCK, BLOCK)
            total[pl.ds(target, BLOCK), :FEAT] += part
        return carry

    lax.fori_loop(0, LIST // 5, step, 0)
    out[...] = pltpu.roll(total[...], spot[1] * FEAT, 1).astype(jnp.bfloat16)


def history_term(listed, order, rows, spot, adj, chunks):
    return pl.pallas_call(
        functools.partial(history_body, len(chunks)),
        out_shape=jax.ShapeDtypeStruct((ROWS * BLOCK, WIDE), jnp.bfloat16),
        grid_spec=pltpu.PrefetchScalarGridSpec(
            num_scalar_prefetch=4,
            grid=(1,),
            in_specs=[pl.BlockSpec(memory_space=pltpu.HBM)] * (1 + len(chunks)),
            out_specs=pl.BlockSpec((ROWS * BLOCK, WIDE), lambda i, *_: (0, 0)),
            scratch_shapes=[
                pltpu.VMEM(adj.shape, jnp.bfloat16),
                pltpu.VMEM((64 * FEAT, HALF), jnp.bfloat16),
                pltpu.VMEM((ROWS * BLOCK, WIDE), jnp.float32),
                pltpu.SemaphoreType.DMA((33,)),
            ],
        ),
        compiler_params=params(16),
        name="history_term",
    )(listed, order, rows, spot, adj, *chunks)


def add_parts(parts):
    def body(parts_ref, out):
        total = parts_ref[0].astype(jnp.float32)
        for k in range(1, parts.shape[0]):
            total = total + parts_ref[k].astype(jnp.float32)
        out[...] = total.astype(jnp.bfloat16)

    return pl.pallas_call(
        body,
        out_shape=jax.ShapeDtypeStruct(parts.shape[1:], jnp.bfloat16),
        compiler_params=params(8),
        name="add_parts",
    )(parts)


def first_dense(halves, weight, spot):
    def body(spot_ref, halves_ref, weight_ref, hidden, chunk):
        rows = [
            jnp.concatenate([halves_ref[0, part], halves_ref[1, part]], axis=1)
            for part in range(2)
        ]
        value = jnp.dot(
            jnp.concatenate(rows, axis=0), weight_ref[...], preferred_element_type=jnp.float32
        )
        value = jnp.maximum(value, 0.0).astype(jnp.bfloat16)
        low = spot_ref[0] == 0
        hidden[...] = jnp.where(low, value[:BLOCK], value[BLOCK:])
        chunk[...] = jnp.where(low, value[:, :HALF], value[:, HALF:])

    return pl.pallas_call(
        body,
        out_shape=(
            jax.ShapeDtypeStruct((BLOCK, F), jnp.bfloat16),
            jax.ShapeDtypeStruct((2 * BLOCK, HALF), jnp.bfloat16),
        ),
        grid_spec=pltpu.PrefetchScalarGridSpec(
            num_scalar_prefetch=1,
            grid=(1,),
            in_specs=[
                pl.BlockSpec(halves.shape, lambda i, *_: (0, 0, 0, 0)),
                pl.BlockSpec(weight.shape, lambda i, *_: (0, 0)),
            ],
            out_specs=(
                pl.BlockSpec((BLOCK, F), lambda i, *_: (0, 0)),
                pl.BlockSpec((2 * BLOCK, HALF), lambda i, *_: (0, 0)),
            ),
        ),
        compiler_params=params(8),
        name="first_dense",
    )(spot, halves, weight)


def second_dense(halves, weight):
    def body(halves_ref, weight_ref, out):
        rows = jnp.concatenate([halves_ref[0], halves_ref[1]], axis=1)
        value = jnp.dot(rows, weight_ref[...], preferred_element_type=jnp.float32)
        out[...] = value.astype(jnp.bfloat16)

    return pl.pallas_call(
        body,
        out_shape=jax.ShapeDtypeStruct((BLOCK, F), jnp.bfloat16),
        compiler_params=params(8),
        name="second_dense",
    )(halves, weight)


def gather_ring(chunk):
    up = [chunk]
    down = [chunk]
    for _ in range(7):
        up.append(lax.ppermute(up[-1], "z", UP))
        down.append(lax.ppermute(down[-1], "z", DOWN))
    half = chunk.shape[0] // 2
    far = [
        lax.ppermute(down[7][:half], "z", DOWN),
        lax.ppermute(up[7][half:], "z", UP),
    ]
    return down + far + up[:0:-1]


def reduce_rows(keep, send):
    other = lax.ppermute(send, "core", SWAP)
    both = (keep.astype(jnp.float32) + other.astype(jnp.float32)).astype(jnp.bfloat16)
    return add_parts(lax.all_to_all(both, SIDE, 0, 0, tiled=True))


def local(
    node_feats,
    adj_vals,
    adj_col,
    adj_count,
    hist_store,
    hist_list,
    hist_adj,
    hist_row,
    hist_col,
    w_first,
    w_second,
):
    adj = adj_vals[0, 0].reshape(ROWS * SLOTS, BLOCK, BLOCK)
    cols = adj_col[0, 0].T
    counts = adj_count[0, 0]
    x_lo = lax.axis_index("x_lo")
    x_hi = lax.axis_index("x_hi")
    grid_index = lax.axis_index(GRID)
    group = jnp.where(x_lo == x_hi, (grid_index // 4) % 2, -1)
    spot = jnp.stack([x_lo, lax.axis_index("core"), group, lax.axis_index("z")])
    spot = spot.astype(jnp.int32)
    hist_spot = jnp.stack([lax.axis_index(DOM), grid_index % 4, lax.axis_index("z")]).astype(jnp.int32)

    payload = make_payload(
        cols,
        counts,
        pltpu.with_memory_space_constraint(node_feats, pltpu.HBM),
        pltpu.with_memory_space_constraint(hist_store, pltpu.HBM),
    )
    received = lax.all_to_all(payload, "x_lo", 0, 0, tiled=True)
    adj_held, received = lax.optimization_barrier((adj, received))
    partner = lax.ppermute(adj_held, "x_lo", SWAP)
    chunks = gather_ring(received[:, :CARRY].reshape(2 * CARRY, HALF))
    chunks = [pltpu.with_memory_space_constraint(chunk, pltpu.HBM) for chunk in chunks]
    partner = pltpu.with_memory_space_constraint(partner, pltpu.HBM)
    adj = pltpu.with_memory_space_constraint(adj, pltpu.HBM)
    theirs = lax.dynamic_index_in_dim(received[:, CARRY, :80], 1 - x_lo, 0, False)
    theirs = theirs.astype(jnp.int32)
    mine = history_term(hist_list, hist_col[0], hist_row[0], hist_spot, hist_adj[0], chunks)

    tables = (cols, counts, theirs, spot)
    agg = reduce_rows(*tile_product(*tables, adj, partner, chunks, ()))
    halves = lax.all_gather(agg, "x_lo", axis=0, tiled=False)
    hidden, chunk = first_dense(halves, w_first, spot)

    chunk, mine = lax.optimization_barrier((chunk, mine))
    extras = (mine, lax.ppermute(mine, "x_lo", SWAP))
    chunks = gather_ring(chunk)
    agg = reduce_rows(*tile_product(*tables, adj, partner, chunks, extras))
    embedding = second_dense(lax.all_to_all(agg, "x_lo", 0, 0, tiled=True), w_second)
    return hidden, embedding


def solution(mesh):
    fine = Mesh(
        mesh.devices.reshape(2, 16, 2, 4, 2), ("x_lo", "z", "x_hi", "y", "core")
    )
    placed = (
        P(DOM + GRID, None),
        P(DOM, GRID),
        P(DOM, GRID),
        P(DOM, GRID),
        P(GRID, DOM),
        P(),
        P(DOM),
        P(DOM),
        P(DOM),
        P(),
        P(),
    )
    return jax.shard_map(
        local,
        mesh=fine,
        in_specs=placed,
        out_specs=(P(DOM + GRID, None), P(DOM + GRID, None)),
        check_vma=False,
    )
```

```python
import functools

import jax
import jax.numpy as jnp
from jax import lax
from jax.experimental import pallas as pl
from jax.experimental.pallas import tpu as pltpu
from jax.sharding import Mesh, PartitionSpec as P

F = 512
HALF = 256
BLOCK = 128
HOWN = 4
ROWS = 16
SLOTS = 4
FEAT = 32
LIST = 40
WIDE = 128
META = 16
PAY = BLOCK + META
FAR = 6
DOM = ("x_lo", "z")
GRID = ("x_hi", "y", "core")
SIDE = ("x_hi", "y")
SWAP = [(0, 1), (1, 0)]


def from_z(value, offset):
    return lax.ppermute(value, "z", [((z + offset) % 16, z) for z in range(16)])


def params(mib):
    return pltpu.CompilerParams(vmem_limit_bytes=mib << 20)


def payload_body(cols, counts, feats, hist, out, own, feats_in, hist_in, sems):
    moves = [
        pltpu.make_async_copy(feats, feats_in, sems.at[0]),
        pltpu.make_async_copy(hist, hist_in, sems.at[1]),
    ]
    for move in moves:
        move.start()
    lane = lax.broadcasted_iota(jnp.int32, (META, HALF), 1)
    meta = jnp.zeros((META, HALF), jnp.float32)
    for row in range(ROWS):
        for slot in range(SLOTS):
            meta = jnp.where(lane == row * SLOTS + slot, cols[slot, row].astype(jnp.float32), meta)
        meta = jnp.where(lane == ROWS * SLOTS + row, counts[row].astype(jnp.float32), meta)
    meta = meta.astype(jnp.bfloat16)
    for move in moves:
        move.wait()
    for j in range(2):
        out[j, :BLOCK] = feats_in[:, j * HALF : (j + 1) * HALF]
        out[j, BLOCK:] = meta
        own[j * FEAT : (j + 1) * FEAT] = hist_in[:, j * HALF : (j + 1) * HALF]


def make_payload(cols, counts, feats, hist):
    return pl.pallas_call(
        payload_body,
        out_shape=(
            jax.ShapeDtypeStruct((2, PAY, HALF), jnp.bfloat16),
            jax.ShapeDtypeStruct((2 * FEAT, HALF), jnp.bfloat16),
        ),
        grid_spec=pltpu.PrefetchScalarGridSpec(
            num_scalar_prefetch=2,
            grid=(1,),
            in_specs=[pl.BlockSpec(memory_space=pltpu.HBM)] * 2,
            out_specs=(
                pl.BlockSpec((2, PAY, HALF), lambda i, *_: (0, 0, 0)),
                pl.BlockSpec((2 * FEAT, HALF), lambda i, *_: (0, 0)),
            ),
            scratch_shapes=[
                pltpu.VMEM(feats.shape, jnp.bfloat16),
                pltpu.VMEM(hist.shape, jnp.bfloat16),
                pltpu.SemaphoreType.DMA((2,)),
            ],
        ),
        compiler_params=params(8),
        name="payload",
    )(cols, counts, feats, hist)


def tile_body(n_chunks, stride, second, cols, counts, theirs, spot, own, partner, *rest):
    chunks = rest[:n_chunks]
    if second:
        extras = rest[n_chunks : n_chunks + 2]
        keep, send, panel, adj, sems, added = rest[-6:]
    else:
        keep, send, store, panel, adj, sems = rest[-6:]
    core = spot[1]
    moves = []

    def move(source, target):
        moves.append(pltpu.make_async_copy(source, target, sems.at[len(moves)]))
        moves[-1].start()

    start = 0
    for source in chunks:
        move(source, panel.at[pl.ds(start, source.shape[0])])
        start += source.shape[0]
    for k, source in enumerate((own, partner)):
        for c in range(4):
            move(source.at[pl.ds(16 * c, 16)], adj.at[pl.ds(64 * k + 16 * c, 16)])
    if second:
        for k in range(2):
            move(extras[k], added.at[k])

    def product(k, row):
        base = (ROWS * k + row) * SLOTS
        count = counts[row] if k == 0 else theirs[ROWS * SLOTS + row]
        left = []
        right = []
        for slot in range(SLOTS):
            block = adj[base + slot]
            left.append(jnp.where(slot < count, block, jnp.zeros_like(block)))
            col = cols[slot, row] if k == 0 else theirs[row * SLOTS + slot]
            place = (((col & 15) - spot[3]) & 15) * stride + (col >> 4) * BLOCK
            right.append(panel[pl.ds(pl.multiple_of(place, 2 * FEAT), BLOCK), :])
        return jnp.dot(
            jnp.concatenate(left, axis=1),
            jnp.concatenate(right, axis=0),
            preferred_element_type=jnp.float32,
        )

    def with_history(k, row, value):
        piece = added[k, row * BLOCK : (row + 1) * BLOCK, :].astype(jnp.float32)
        zero = jnp.zeros_like(piece)
        wide = [jnp.where(spot[2] == group, piece, zero) for group in range(2)]
        return value + jnp.concatenate(wide, axis=1)

    def two_rows(k, j):
        part = spot[0] if k == 0 else 1 - spot[0]
        pair = [product(k, 2 * j + side) for side in range(2)]
        if second:
            pair = [with_history(k, 2 * j + side, pair[side]) for side in range(2)]
        even, odd = [value.astype(jnp.bfloat16) for value in pair]
        keep[j, part] = jnp.where(core == 0, even, odd)
        send[j, part] = jnp.where(core == 0, odd, even)

    for n in range(n_chunks):
        moves[n].wait()
    if not second:
        for d in range(16):
            source = panel.at[pl.ds(d * stride + 2 * BLOCK, 2 * FEAT)]
            move(source, store.at[pl.ds(d * 2 * FEAT, 2 * FEAT)])
    for k in range(2):
        for c in range(4):
            moves[n_chunks + 4 * k + c].wait()
            if second and c == 0:
                moves[n_chunks + 8 + k].wait()
            two_rows(k, 2 * c)
            two_rows(k, 2 * c + 1)
    if not second:
        for d in range(16):
            moves[n_chunks + 8 + d].wait()


def tile_product(cols, counts, theirs, spot, own, partner, chunks, extras):
    operands = [own, partner, *chunks, *extras]
    stride = chunks[0].shape[0]
    second = bool(extras)
    half = jax.ShapeDtypeStruct((ROWS // 2, 2, BLOCK, HALF), jnp.bfloat16)
    outs = [half, half]
    out_specs = [pl.BlockSpec(half.shape, lambda i, *_: (0, 0, 0, 0))] * 2
    scratch = [
        pltpu.VMEM((16 * stride, HALF), jnp.bfloat16),
        pltpu.VMEM((2 * ROWS * SLOTS, BLOCK, BLOCK), jnp.bfloat16),
        pltpu.SemaphoreType.DMA((len(chunks) + 8 + (2 if second else 16),)),
    ]
    if second:
        scratch.append(pltpu.VMEM((2, ROWS * BLOCK, WIDE), jnp.bfloat16))
    else:
        outs.append(jax.ShapeDtypeStruct((32 * FEAT, HALF), jnp.bfloat16))
        out_specs.append(pl.BlockSpec(memory_space=pltpu.HBM))
    return pl.pallas_call(
        functools.partial(tile_body, len(chunks), stride, second),
        out_shape=tuple(outs),
        grid_spec=pltpu.PrefetchScalarGridSpec(
            num_scalar_prefetch=4,
            grid=(1,),
            in_specs=[pl.BlockSpec(memory_space=pltpu.HBM)] * len(operands),
            out_specs=tuple(out_specs),
            scratch_shapes=scratch,
        ),
        compiler_params=params(20),
        name="tile_product",
    )(cols, counts, theirs, spot, *operands)


def history_body(listed, order, rows, spot, adj, same, other, out, weights, store, total, sems):
    moves = [
        pltpu.make_async_copy(adj, weights, sems.at[0]),
        pltpu.make_async_copy(same, store.at[0], sems.at[1]),
        pltpu.make_async_copy(other, store.at[1], sems.at[2]),
    ]
    for move in moves:
        move.start()
    total[...] = jnp.zeros_like(total)
    for move in moves:
        move.wait()

    def one(slot):
        block = listed[spot[0], order[slot]]
        owner = block >> 2
        piece = block & 3
        place = (((owner & 15) - spot[2]) & 15) * (2 * FEAT) + (piece >> 1) * FEAT
        source = pl.multiple_of(place, FEAT)
        lane = pl.multiple_of((piece & 1) * BLOCK, BLOCK)
        return lax.dot_general(
            weights[slot],
            store[(owner >> 4) ^ spot[3], pl.ds(source, FEAT), pl.ds(lane, BLOCK)],
            (((1,), (1,)), ((), ())),
            preferred_element_type=jnp.float32,
        )

    def step(n, carry):
        parts = [one(n * 5 + k) for k in range(5)]
        for k, part in enumerate(parts):
            target = pl.multiple_of(rows[n * 5 + k] * BLOCK, BLOCK)
            total[pl.ds(target, BLOCK), :FEAT] += part
        return carry

    lax.fori_loop(0, LIST // 5, step, 0)
    out[...] = pltpu.roll(total[...], spot[1] * FEAT, 1).astype(jnp.bfloat16)


def history_term(listed, order, rows, spot, adj, same, other):
    return pl.pallas_call(
        history_body,
        out_shape=jax.ShapeDtypeStruct((ROWS * BLOCK, WIDE), jnp.bfloat16),
        grid_spec=pltpu.PrefetchScalarGridSpec(
            num_scalar_prefetch=4,
            grid=(1,),
            in_specs=[pl.BlockSpec(memory_space=pltpu.HBM)] * 3,
            out_specs=pl.BlockSpec((ROWS * BLOCK, WIDE), lambda i, *_: (0, 0)),
            scratch_shapes=[
                pltpu.VMEM(adj.shape, jnp.bfloat16),
                pltpu.VMEM((2, *same.shape), jnp.bfloat16),
                pltpu.VMEM((ROWS * BLOCK, WIDE), jnp.float32),
                pltpu.SemaphoreType.DMA((3,)),
            ],
        ),
        compiler_params=params(16),
        name="history_term",
    )(listed, order, rows, spot, adj, same, other)


def add_parts(parts):
    def body(parts_ref, out):
        total = parts_ref[0].astype(jnp.float32)
        for k in range(1, parts.shape[0]):
            total = total + parts_ref[k].astype(jnp.float32)
        out[...] = total.astype(jnp.bfloat16)

    return pl.pallas_call(
        body,
        out_shape=jax.ShapeDtypeStruct(parts.shape[1:], jnp.bfloat16),
        compiler_params=params(8),
        name="add_parts",
    )(parts)


def first_dense(halves, weight, spot):
    def body(spot_ref, halves_ref, weight_ref, hidden, chunk):
        rows = [
            jnp.concatenate([halves_ref[0, part], halves_ref[1, part]], axis=1)
            for part in range(2)
        ]
        value = jnp.dot(
            jnp.concatenate(rows, axis=0), weight_ref[...], preferred_element_type=jnp.float32
        )
        value = jnp.maximum(value, 0.0).astype(jnp.bfloat16)
        low = spot_ref[0] == 0
        hidden[...] = jnp.where(low, value[:BLOCK], value[BLOCK:])
        chunk[...] = jnp.where(low, value[:, :HALF], value[:, HALF:])

    return pl.pallas_call(
        body,
        out_shape=(
            jax.ShapeDtypeStruct((BLOCK, F), jnp.bfloat16),
            jax.ShapeDtypeStruct((2 * BLOCK, HALF), jnp.bfloat16),
        ),
        grid_spec=pltpu.PrefetchScalarGridSpec(
            num_scalar_prefetch=1,
            grid=(1,),
            in_specs=[
                pl.BlockSpec(halves.shape, lambda i, *_: (0, 0, 0, 0)),
                pl.BlockSpec(weight.shape, lambda i, *_: (0, 0)),
            ],
            out_specs=(
                pl.BlockSpec((BLOCK, F), lambda i, *_: (0, 0)),
                pl.BlockSpec((2 * BLOCK, HALF), lambda i, *_: (0, 0)),
            ),
        ),
        compiler_params=params(8),
        name="first_dense",
    )(spot, halves, weight)


def second_dense(halves, weight):
    def body(halves_ref, weight_ref, out):
        rows = jnp.concatenate([halves_ref[0], halves_ref[1]], axis=1)
        value = jnp.dot(rows, weight_ref[...], preferred_element_type=jnp.float32)
        out[...] = value.astype(jnp.bfloat16)

    return pl.pallas_call(
        body,
        out_shape=jax.ShapeDtypeStruct((BLOCK, F), jnp.bfloat16),
        compiler_params=params(8),
        name="second_dense",
    )(halves, weight)


def gather_ring(chunk):
    ahead = {0: chunk}
    behind = {0: chunk}
    far_ahead = from_z(chunk, FAR)
    far_behind = from_z(chunk, -FAR)
    for d in range(1, FAR):
        ahead[d] = from_z(ahead[d - 1], 1)
        behind[d] = from_z(behind[d - 1], -1)
        if d == 3:
            far_ahead, ahead[3] = lax.optimization_barrier((far_ahead, ahead[3]))
            far_behind, behind[3] = lax.optimization_barrier((far_behind, behind[3]))
            ahead[FAR] = far_ahead
            behind[FAR] = far_behind
    ahead[7] = from_z(ahead[6], 1)
    behind[7] = from_z(behind[6], -1)
    half = chunk.shape[0] // 2
    across = [from_z(ahead[7][:half], 1), from_z(behind[7][half:], -1)]
    return [ahead[d] for d in range(8)] + across + [behind[d] for d in range(7, 0, -1)]


def reduce_rows(keep, send):
    other = lax.ppermute(send, "core", SWAP)
    both = (keep.astype(jnp.float32) + other.astype(jnp.float32)).astype(jnp.bfloat16)
    return add_parts(lax.all_to_all(both, SIDE, 0, 0, tiled=True))


def local(
    node_feats,
    adj_vals,
    adj_col,
    adj_count,
    hist_store,
    hist_list,
    hist_adj,
    hist_row,
    hist_col,
    w_first,
    w_second,
):
    adj = adj_vals[0, 0].reshape(ROWS * SLOTS, BLOCK, BLOCK)
    cols = adj_col[0, 0].T
    counts = adj_count[0, 0]
    x_lo = lax.axis_index("x_lo")
    x_hi = lax.axis_index("x_hi")
    grid_index = lax.axis_index(GRID)
    group = jnp.where(x_lo == x_hi, (grid_index // 4) % 2, -1)
    spot = jnp.stack([x_lo, lax.axis_index("core"), group, lax.axis_index("z")])
    spot = spot.astype(jnp.int32)
    hist_spot = jnp.stack([lax.axis_index(DOM), grid_index % 4, lax.axis_index("z"), x_lo])
    hist_spot = hist_spot.astype(jnp.int32)

    payload, own_store = make_payload(
        cols,
        counts,
        pltpu.with_memory_space_constraint(node_feats, pltpu.HBM),
        pltpu.with_memory_space_constraint(hist_store, pltpu.HBM),
    )
    received = lax.all_to_all(payload, "x_lo", 0, 0, tiled=True)
    adj_held, received = lax.optimization_barrier((adj, received))
    partner = lax.ppermute(adj_held, "x_lo", SWAP)
    chunk = jnp.concatenate([received[0, :BLOCK], received[1, :BLOCK], own_store], axis=0)
    chunks = gather_ring(chunk)
    chunks = [pltpu.with_memory_space_constraint(chunk, pltpu.HBM) for chunk in chunks]
    partner = pltpu.with_memory_space_constraint(partner, pltpu.HBM)
    adj = pltpu.with_memory_space_constraint(adj, pltpu.HBM)
    theirs = lax.dynamic_index_in_dim(received[:, BLOCK, :80], 1 - x_lo, 0, False)
    tables = (cols, counts, theirs.astype(jnp.int32), spot)

    keep, send, store = tile_product(*tables, adj, partner, chunks, ())
    agg = reduce_rows(keep, send)
    other_store = lax.ppermute(store, "x_lo", SWAP)
    mine = history_term(
        hist_list, hist_col[0], hist_row[0], hist_spot, hist_adj[0], store, other_store
    )
    halves = lax.all_gather(agg, "x_lo", axis=0, tiled=False)
    hidden, chunk = first_dense(halves, w_first, spot)

    extras = (mine, lax.ppermute(mine, "x_lo", SWAP))
    chunks = gather_ring(chunk)
    agg = reduce_rows(*tile_product(*tables, adj, partner, chunks, extras))
    embedding = second_dense(lax.all_to_all(agg, "x_lo", 0, 0, tiled=True), w_second)
    return hidden, embedding


def solution(mesh):
    fine = Mesh(
        mesh.devices.reshape(2, 16, 2, 4, 2), ("x_lo", "z", "x_hi", "y", "core")
    )
    placed = (
        P(DOM + GRID, None),
        P(DOM, GRID),
        P(DOM, GRID),
        P(DOM, GRID),
        P(GRID, DOM),
        P(),
        P(DOM),
        P(DOM),
        P(DOM),
        P(),
        P(),
    )
    return jax.shard_map(
        local,
        mesh=fine,
        in_specs=placed,
        out_specs=(P(DOM + GRID, None), P(DOM + GRID, None)),
        check_vma=False,
    )
```

```python
import functools

import jax
import jax.numpy as jnp
from jax import lax
from jax.experimental import pallas as pl
from jax.experimental.pallas import tpu as pltpu
from jax.sharding import Mesh, PartitionSpec as P

F = 512
HALF = 256
BLOCK = 128
HOWN = 4
ROWS = 16
SLOTS = 4
FEAT = 32
LIST = 40
WIDE = 128
DOM = ("x_lo", "zq", "zr")
Z = ("zq", "zr")
GRID = ("x_hi", "y", "core")
SIDE = ("x_hi", "y")
SWAP = [(0, 1), (1, 0)]


def from_z(value, offset):
    return lax.ppermute(value, Z, [((z + offset) % 16, z) for z in range(16)])


def params(mib):
    return pltpu.CompilerParams(vmem_limit_bytes=mib << 20)


def tile_body(second, n_chunks, cols, counts, theirs, spot, *rest):
    n_parts = 2 if second else 1
    tiles = rest[:n_parts]
    chunks = rest[n_parts : n_parts + n_chunks]
    if second:
        extras = rest[n_parts + n_chunks : n_parts + n_chunks + 2]
        keep, send, panel, adj, sems, added = rest[-6:]
    else:
        keep, send, panel, adj, sems = rest[-5:]
    core = spot[1]
    moves = []

    def move(source, target):
        moves.append(pltpu.make_async_copy(source, target, sems.at[len(moves)]))
        moves[-1].start()

    start = 0
    for source in chunks:
        move(source, panel.at[pl.ds(start, source.shape[0])])
        start += source.shape[0]
    for k in range(n_parts):
        for c in range(4):
            move(tiles[k].at[pl.ds(16 * c, 16)], adj.at[pl.ds(64 * k + 16 * c, 16)])
    if second:
        for k in range(2):
            move(extras[k], added.at[k])

    def product(k, row):
        base = (ROWS * k + row) * SLOTS
        count = counts[row] if k == 0 else theirs[ROWS * SLOTS + row]
        left = []
        right = []
        for slot in range(SLOTS):
            block = adj[base + slot]
            left.append(jnp.where(slot < count, block, jnp.zeros_like(block)))
            col = cols[slot, row] if k == 0 else theirs[row * SLOTS + slot]
            z = col & 15
            index = ((z - spot[3]) & 3) * 4 + (z >> 2) if second else z
            start = pl.multiple_of((index * 2 + (col >> 4)) * BLOCK, BLOCK)
            right.append(panel[pl.ds(start, BLOCK), :])
        return jnp.dot(
            jnp.concatenate(left, axis=1),
            jnp.concatenate(right, axis=0),
            preferred_element_type=jnp.float32,
        )

    def with_history(k, row, value):
        piece = added[k, row * BLOCK : (row + 1) * BLOCK, :].astype(jnp.float32)
        zero = jnp.zeros_like(piece)
        wide = [jnp.where(spot[2] == group, piece, zero) for group in range(2)]
        return value + jnp.concatenate(wide, axis=1)

    def two_rows(k, j):
        pair = [product(k, 2 * j + side) for side in range(2)]
        if second:
            pair = [with_history(k, 2 * j + side, pair[side]) for side in range(2)]
        even, odd = [value.astype(jnp.bfloat16) for value in pair]
        part = spot[0] if k == 0 else 1 - spot[0]
        where = (j, part) if second else (j,)
        keep[where] = jnp.where(core == 0, even, odd)
        send[where] = jnp.where(core == 0, odd, even)

    for n in range(n_chunks):
        moves[n].wait()
    for k in range(n_parts):
        for c in range(4):
            moves[n_chunks + 4 * k + c].wait()
            if second and c == 0:
                moves[n_chunks + 8 + k].wait()
            two_rows(k, 2 * c)
            two_rows(k, 2 * c + 1)


def tile_product(cols, counts, theirs, spot, tiles, chunks, extras):
    operands = [*tiles, *chunks, *extras]
    second = bool(extras)
    width = chunks[0].shape[1]
    shape = (ROWS // 2, 2, BLOCK, width) if second else (ROWS // 2, BLOCK, width)
    half = jax.ShapeDtypeStruct(shape, jnp.bfloat16)
    scratch = [
        pltpu.VMEM((32 * BLOCK, width), jnp.bfloat16),
        pltpu.VMEM((len(tiles) * ROWS * SLOTS, BLOCK, BLOCK), jnp.bfloat16),
        pltpu.SemaphoreType.DMA((len(chunks) + 4 * len(tiles) + len(extras),)),
    ]
    if second:
        scratch.append(pltpu.VMEM((2, ROWS * BLOCK, WIDE), jnp.bfloat16))
    out_spec = pl.BlockSpec(shape, lambda i, *_: (0,) * len(shape))
    return pl.pallas_call(
        functools.partial(tile_body, second, len(chunks)),
        out_shape=(half, half),
        grid_spec=pltpu.PrefetchScalarGridSpec(
            num_scalar_prefetch=4,
            grid=(1,),
            in_specs=[pl.BlockSpec(memory_space=pltpu.HBM)] * len(operands),
            out_specs=(out_spec, out_spec),
            scratch_shapes=scratch,
        ),
        compiler_params=params(20),
        name="tile_product",
    )(cols, counts, theirs, spot, *operands)


def history_body(listed, order, rows, spot, adj, same, other, out, weights, store, total, sems):
    moves = [
        pltpu.make_async_copy(adj, weights, sems.at[0]),
        pltpu.make_async_copy(same, store.at[0], sems.at[1]),
        pltpu.make_async_copy(other, store.at[1], sems.at[2]),
    ]
    for move in moves:
        move.start()
    total[...] = jnp.zeros_like(total)
    for move in moves:
        move.wait()

    def one(slot):
        block = listed[spot[0], order[slot]]
        owner = block >> 2
        piece = block & 3
        source = pl.multiple_of((owner & 15) * FEAT, FEAT)
        lane = pl.multiple_of(piece * BLOCK, BLOCK)
        return lax.dot_general(
            weights[slot],
            store[(owner >> 4) ^ spot[2], pl.ds(source, FEAT), pl.ds(lane, BLOCK)],
            (((1,), (1,)), ((), ())),
            preferred_element_type=jnp.float32,
        )

    def step(n, carry):
        parts = [one(n * 5 + k) for k in range(5)]
        for k, part in enumerate(parts):
            target = pl.multiple_of(rows[n * 5 + k] * BLOCK, BLOCK)
            total[pl.ds(target, BLOCK), :FEAT] += part
        return carry

    lax.fori_loop(0, LIST // 5, step, 0)
    out[...] = pltpu.roll(total[...], spot[1] * FEAT, 1).astype(jnp.bfloat16)


def history_term(listed, order, rows, spot, adj, same, other):
    return pl.pallas_call(
        history_body,
        out_shape=jax.ShapeDtypeStruct((ROWS * BLOCK, WIDE), jnp.bfloat16),
        grid_spec=pltpu.PrefetchScalarGridSpec(
            num_scalar_prefetch=4,
            grid=(1,),
            in_specs=[pl.BlockSpec(memory_space=pltpu.HBM)] * 3,
            out_specs=pl.BlockSpec((ROWS * BLOCK, WIDE), lambda i, *_: (0, 0)),
            scratch_shapes=[
                pltpu.VMEM(adj.shape, jnp.bfloat16),
                pltpu.VMEM((2, *same.shape), jnp.bfloat16),
                pltpu.VMEM((ROWS * BLOCK, WIDE), jnp.float32),
                pltpu.SemaphoreType.DMA((3,)),
            ],
        ),
        compiler_params=params(16),
        name="history_term",
    )(listed, order, rows, spot, adj, same, other)


def add_parts(parts):
    def body(parts_ref, out):
        total = parts_ref[0].astype(jnp.float32)
        for k in range(1, parts.shape[0]):
            total = total + parts_ref[k].astype(jnp.float32)
        out[...] = total.astype(jnp.bfloat16)

    return pl.pallas_call(
        body,
        out_shape=jax.ShapeDtypeStruct(parts.shape[1:], jnp.bfloat16),
        compiler_params=params(8),
        name="add_parts",
    )(parts)


def first_dense(parts, weight):
    def body(parts_ref, weight_ref, hidden, halves):
        total = parts_ref[0].astype(jnp.float32)
        for k in range(1, parts.shape[0]):
            total = total + parts_ref[k].astype(jnp.float32)
        value = jnp.dot(
            total.astype(jnp.bfloat16), weight_ref[...], preferred_element_type=jnp.float32
        )
        value = jnp.maximum(value, 0.0).astype(jnp.bfloat16)
        hidden[...] = value
        halves[0] = value[:, :HALF]
        halves[1] = value[:, HALF:]

    return pl.pallas_call(
        body,
        out_shape=(
            jax.ShapeDtypeStruct((BLOCK, F), jnp.bfloat16),
            jax.ShapeDtypeStruct((2, BLOCK, HALF), jnp.bfloat16),
        ),
        compiler_params=params(8),
        name="first_dense",
    )(parts, weight)


def second_dense(halves, weight):
    def body(halves_ref, weight_ref, out):
        rows = jnp.concatenate([halves_ref[0], halves_ref[1]], axis=1)
        value = jnp.dot(rows, weight_ref[...], preferred_element_type=jnp.float32)
        out[...] = value.astype(jnp.bfloat16)

    return pl.pallas_call(
        body,
        out_shape=jax.ShapeDtypeStruct((BLOCK, F), jnp.bfloat16),
        compiler_params=params(8),
        name="second_dense",
    )(halves, weight)


def gather_quads(chunk):
    same = lax.all_gather(chunk, "zq", axis=0, tiled=True)
    above = from_z(same, 1)
    below = from_z(same, -1)
    half = same.shape[0] // 2
    across = [from_z(above[:half], 1), from_z(below[half:], -1)]
    return [same, above, *across, below]


def reduce_rows(keep, send):
    other = lax.ppermute(send, "core", SWAP)
    both = (keep.astype(jnp.float32) + other.astype(jnp.float32)).astype(jnp.bfloat16)
    return lax.all_to_all(both, SIDE, 0, 0, tiled=True)


def local(
    node_feats,
    adj_vals,
    adj_col,
    adj_count,
    hist_store,
    hist_list,
    hist_adj,
    hist_row,
    hist_col,
    w_first,
    w_second,
):
    adj = adj_vals[0, 0].reshape(ROWS * SLOTS, BLOCK, BLOCK)
    cols = adj_col[0, 0].T
    counts = adj_count[0, 0]
    x_lo = lax.axis_index("x_lo")
    x_hi = lax.axis_index("x_hi")
    grid_index = lax.axis_index(GRID)
    group = jnp.where(x_lo == x_hi, (grid_index // 4) % 2, -1)
    spot = jnp.stack([x_lo, lax.axis_index("core"), group, lax.axis_index(Z)])
    spot = spot.astype(jnp.int32)
    hist_spot = jnp.stack([lax.axis_index(DOM), grid_index % 4, x_lo]).astype(jnp.int32)

    pair = lax.all_gather(node_feats, "x_lo", axis=0, tiled=True)
    panel = lax.all_gather(pair, Z, axis=0, tiled=True)

    numbers = jnp.concatenate([adj_col[0, 0].reshape(-1), counts])
    pair, numbers = lax.optimization_barrier((pair, numbers))
    both = lax.all_gather(numbers, "x_lo", axis=0, tiled=False)
    theirs = lax.dynamic_index_in_dim(both, 1 - x_lo, 0, keepdims=False)
    adj_held, theirs = lax.optimization_barrier((adj, theirs))
    partner = lax.ppermute(adj_held, "x_lo", SWAP)

    store = lax.all_gather(hist_store, Z, axis=0, tiled=True)
    store, partner = lax.optimization_barrier((store, partner))
    other_store = lax.ppermute(store, "x_lo", SWAP)
    mine = history_term(
        hist_list, hist_col[0], hist_row[0], hist_spot, hist_adj[0], store, other_store
    )
    extras = (mine, lax.ppermute(mine, "x_lo", SWAP))
    panel, extras = lax.optimization_barrier((panel, extras))

    adj = pltpu.with_memory_space_constraint(adj, pltpu.HBM)
    panel = pltpu.with_memory_space_constraint(panel, pltpu.HBM)
    tables = (cols, counts, theirs, spot)
    parts = reduce_rows(*tile_product(*tables, (adj,), (panel,), ()))
    hidden, halves = first_dense(parts, w_first)

    chunk = lax.all_to_all(halves, "x_lo", 0, 0, tiled=True).reshape(2 * BLOCK, HALF)
    chunks = gather_quads(chunk)
    parts = reduce_rows(*tile_product(*tables, (adj, partner), chunks, extras))
    halves = lax.all_to_all(add_parts(parts), "x_lo", 0, 0, tiled=True)
    return hidden, second_dense(halves, w_second)


def solution(mesh):
    fine = Mesh(
        mesh.devices.reshape(2, 4, 4, 2, 4, 2), ("x_lo", "zq", "zr", "x_hi", "y", "core")
    )
    placed = (
        P(DOM + GRID, None),
        P(DOM, GRID),
        P(DOM, GRID),
        P(DOM, GRID),
        P(GRID, DOM),
        P(),
        P(DOM),
        P(DOM),
        P(DOM),
        P(),
        P(),
    )
    return jax.shard_map(
        local,
        mesh=fine,
        in_specs=placed,
        out_specs=(P(DOM + GRID, None), P(DOM + GRID, None)),
        check_vma=False,
    )
```

```python
import functools

import jax
import jax.numpy as jnp
from jax import lax
from jax.experimental import pallas as pl
from jax.experimental.pallas import tpu as pltpu
from jax.sharding import Mesh, PartitionSpec as P

F = 512
HALF = 256
BLOCK = 128
HOWN = 4
ROWS = 16
SLOTS = 4
FEAT = 32
LIST = 40
WIDE = 128
META = 16
CARRY = BLOCK + 2 * FEAT
PAY = CARRY + META
DOM = ("x_lo", "zq", "zr")
Z = ("zq", "zr")
GRID = ("x_hi", "y", "core")
SIDE = ("x_hi", "y")
ALL_SIDE = ("x_lo", "x_hi", "y")
SWAP = [(0, 1), (1, 0)]


def from_z(value, offset):
    return lax.ppermute(value, Z, [((z + offset) % 16, z) for z in range(16)])


def params(mib):
    return pltpu.CompilerParams(vmem_limit_bytes=mib << 20)


def payload_body(cols, counts, feats, hist, out, feats_in, hist_in, sems):
    moves = [
        pltpu.make_async_copy(feats, feats_in, sems.at[0]),
        pltpu.make_async_copy(hist, hist_in, sems.at[1]),
    ]
    for move in moves:
        move.start()
    lane = lax.broadcasted_iota(jnp.int32, (META, HALF), 1)
    meta = jnp.zeros((META, HALF), jnp.float32)
    for row in range(ROWS):
        for slot in range(SLOTS):
            meta = jnp.where(lane == row * SLOTS + slot, cols[slot, row].astype(jnp.float32), meta)
        meta = jnp.where(lane == ROWS * SLOTS + row, counts[row].astype(jnp.float32), meta)
    meta = meta.astype(jnp.bfloat16)
    for move in moves:
        move.wait()
    for j in range(2):
        out[j, :BLOCK] = feats_in[:, j * HALF : (j + 1) * HALF]
        for k in range(2):
            start = BLOCK + k * FEAT
            out[j, start : start + FEAT] = hist_in[:, k * HALF : (k + 1) * HALF]
        out[j, CARRY:] = meta


def make_payload(cols, counts, feats, hist):
    return pl.pallas_call(
        payload_body,
        out_shape=jax.ShapeDtypeStruct((2, PAY, HALF), jnp.bfloat16),
        grid_spec=pltpu.PrefetchScalarGridSpec(
            num_scalar_prefetch=2,
            grid=(1,),
            in_specs=[pl.BlockSpec(memory_space=pltpu.HBM)] * 2,
            out_specs=pl.BlockSpec((2, PAY, HALF), lambda i, *_: (0, 0, 0)),
            scratch_shapes=[
                pltpu.VMEM(feats.shape, jnp.bfloat16),
                pltpu.VMEM(hist.shape, jnp.bfloat16),
                pltpu.SemaphoreType.DMA((2,)),
            ],
        ),
        compiler_params=params(8),
        name="payload",
    )(cols, counts, feats, hist)


def tile_body(second, stride, n_chunks, cols, counts, theirs, spot, *rest):
    tiles = rest[:2]
    chunks = rest[2 : 2 + n_chunks]
    if second:
        extras = rest[2 + n_chunks : 4 + n_chunks]
        keep, send, panel, adj, sems, added = rest[-6:]
    else:
        keep, send, panel, adj, sems = rest[-5:]
    core = spot[1]
    moves = []

    def move(source, target):
        moves.append(pltpu.make_async_copy(source, target, sems.at[len(moves)]))
        moves[-1].start()

    start = 0
    for source in chunks:
        move(source, panel.at[pl.ds(start, source.shape[0])])
        start += source.shape[0]
    for k in range(2):
        for c in range(4):
            move(tiles[k].at[pl.ds(16 * c, 16)], adj.at[pl.ds(64 * k + 16 * c, 16)])
    if second:
        for k in range(2):
            move(extras[k], added.at[k])

    def product(k, row):
        base = (ROWS * k + row) * SLOTS
        count = counts[row] if k == 0 else theirs[ROWS * SLOTS + row]
        left = []
        right = []
        for slot in range(SLOTS):
            block = adj[base + slot]
            left.append(jnp.where(slot < count, block, jnp.zeros_like(block)))
            col = cols[slot, row] if k == 0 else theirs[row * SLOTS + slot]
            z = col & 15
            ahead = z - spot[3]
            index = (ahead & 3) * 4 + (z >> 2) if second else ahead & 15
            start = pl.multiple_of((index * 2 + (col >> 4)) * stride, 2 * FEAT)
            right.append(panel[pl.ds(start, BLOCK), :])
        return jnp.dot(
            jnp.concatenate(left, axis=1),
            jnp.concatenate(right, axis=0),
            preferred_element_type=jnp.float32,
        )

    def with_history(k, row, value):
        piece = added[k, row * BLOCK : (row + 1) * BLOCK, :].astype(jnp.float32)
        zero = jnp.zeros_like(piece)
        wide = [jnp.where(spot[2] == group, piece, zero) for group in range(2)]
        return value + jnp.concatenate(wide, axis=1)

    def two_rows(k, j):
        pair = [product(k, 2 * j + side) for side in range(2)]
        if second:
            pair = [with_history(k, 2 * j + side, pair[side]) for side in range(2)]
        even, odd = [value.astype(jnp.bfloat16) for value in pair]
        part = spot[0] if k == 0 else 1 - spot[0]
        where = (part, j) if second else (j, part)
        keep[where] = jnp.where(core == 0, even, odd)
        send[where] = jnp.where(core == 0, odd, even)

    for n in range(n_chunks):
        moves[n].wait()
    for k in range(2):
        for c in range(4):
            moves[n_chunks + 4 * k + c].wait()
            if second and c == 0:
                moves[n_chunks + 8 + k].wait()
            two_rows(k, 2 * c)
            two_rows(k, 2 * c + 1)


def tile_product(cols, counts, theirs, spot, tiles, chunks, extras):
    operands = [*tiles, *chunks, *extras]
    second = bool(extras)
    stride = sum(chunk.shape[0] for chunk in chunks) // 32
    shape = (2, ROWS // 2, BLOCK, HALF) if second else (ROWS // 2, 2, BLOCK, HALF)
    half = jax.ShapeDtypeStruct(shape, jnp.bfloat16)
    scratch = [
        pltpu.VMEM((32 * stride, HALF), jnp.bfloat16),
        pltpu.VMEM((2 * ROWS * SLOTS, BLOCK, BLOCK), jnp.bfloat16),
        pltpu.SemaphoreType.DMA((len(chunks) + 8 + len(extras),)),
    ]
    if second:
        scratch.append(pltpu.VMEM((2, ROWS * BLOCK, WIDE), jnp.bfloat16))
    out_spec = pl.BlockSpec(shape, lambda i, *_: (0,) * len(shape))
    return pl.pallas_call(
        functools.partial(tile_body, second, stride, len(chunks)),
        out_shape=(half, half),
        grid_spec=pltpu.PrefetchScalarGridSpec(
            num_scalar_prefetch=4,
            grid=(1,),
            in_specs=[pl.BlockSpec(memory_space=pltpu.HBM)] * len(operands),
            out_specs=(out_spec, out_spec),
            scratch_shapes=scratch,
        ),
        compiler_params=params(20),
        name="tile_product",
    )(cols, counts, theirs, spot, *operands)


def history_body(n_chunks, listed, order, rows, spot, adj, *rest):
    chunks = rest[:n_chunks]
    out, weights, store, total, sems = rest[n_chunks:]
    moves = [pltpu.make_async_copy(adj, weights, sems.at[0])]
    start = 0
    for source in chunks:
        for k in range(source.shape[0] // CARRY):
            moves.append(
                pltpu.make_async_copy(
                    source.at[pl.ds(k * CARRY + BLOCK, 2 * FEAT)],
                    store.at[pl.ds(start, 2 * FEAT)],
                    sems.at[len(moves)],
                )
            )
            start += 2 * FEAT
    for move in moves:
        move.start()
    total[...] = jnp.zeros_like(total)
    for move in moves:
        move.wait()

    def one(slot):
        block = listed[spot[0], order[slot]]
        owner = block >> 2
        piece = block & 3
        place = (((owner & 15) - spot[2]) & 15) * 2 + (owner >> 4)
        source = pl.multiple_of(place * (2 * FEAT) + (piece >> 1) * FEAT, FEAT)
        lane = pl.multiple_of((piece & 1) * BLOCK, BLOCK)
        return lax.dot_general(
            weights[slot],
            store[pl.ds(source, FEAT), pl.ds(lane, BLOCK)],
            (((1,), (1,)), ((), ())),
            preferred_element_type=jnp.float32,
        )

    def step(n, carry):
        parts = [one(n * 5 + k) for k in range(5)]
        for k, part in enumerate(parts):
            target = pl.multiple_of(rows[n * 5 + k] * BLOCK, BLOCK)
            total[pl.ds(target, BLOCK), :FEAT] += part
        return carry

    lax.fori_loop(0, LIST // 5, step, 0)
    out[...] = pltpu.roll(total[...], spot[1] * FEAT, 1).astype(jnp.bfloat16)


def history_term(listed, order, rows, spot, adj, chunks):
    return pl.pallas_call(
        functools.partial(history_body, len(chunks)),
        out_shape=jax.ShapeDtypeStruct((ROWS * BLOCK, WIDE), jnp.bfloat16),
        grid_spec=pltpu.PrefetchScalarGridSpec(
            num_scalar_prefetch=4,
            grid=(1,),
            in_specs=[pl.BlockSpec(memory_space=pltpu.HBM)] * (1 + len(chunks)),
            out_specs=pl.BlockSpec((ROWS * BLOCK, WIDE), lambda i, *_: (0, 0)),
            scratch_shapes=[
                pltpu.VMEM(adj.shape, jnp.bfloat16),
                pltpu.VMEM((64 * FEAT, HALF), jnp.bfloat16),
                pltpu.VMEM((ROWS * BLOCK, WIDE), jnp.float32),
                pltpu.SemaphoreType.DMA((33,)),
            ],
        ),
        compiler_params=params(16),
        name="history_term",
    )(listed, order, rows, spot, adj, *chunks)


def add_parts(parts):
    def body(parts_ref, out):
        total = parts_ref[0].astype(jnp.float32)
        for k in range(1, parts.shape[0]):
            total = total + parts_ref[k].astype(jnp.float32)
        out[...] = total.astype(jnp.bfloat16)

    return pl.pallas_call(
        body,
        out_shape=jax.ShapeDtypeStruct(parts.shape[1:], jnp.bfloat16),
        compiler_params=params(8),
        name="add_parts",
    )(parts)


def first_dense(halves, weight, spot):
    def body(spot_ref, halves_ref, weight_ref, hidden, chunk):
        rows = [
            jnp.concatenate([halves_ref[0, part], halves_ref[1, part]], axis=1)
            for part in range(2)
        ]
        value = jnp.dot(
            jnp.concatenate(rows, axis=0), weight_ref[...], preferred_element_type=jnp.float32
        )
        value = jnp.maximum(value, 0.0).astype(jnp.bfloat16)
        low = spot_ref[0] == 0
        hidden[...] = jnp.where(low, value[:BLOCK], value[BLOCK:])
        chunk[...] = jnp.where(low, value[:, :HALF], value[:, HALF:])

    return pl.pallas_call(
        body,
        out_shape=(
            jax.ShapeDtypeStruct((BLOCK, F), jnp.bfloat16),
            jax.ShapeDtypeStruct((2 * BLOCK, HALF), jnp.bfloat16),
        ),
        grid_spec=pltpu.PrefetchScalarGridSpec(
            num_scalar_prefetch=1,
            grid=(1,),
            in_specs=[
                pl.BlockSpec(halves.shape, lambda i, *_: (0, 0, 0, 0)),
                pl.BlockSpec(weight.shape, lambda i, *_: (0, 0)),
            ],
            out_specs=(
                pl.BlockSpec((BLOCK, F), lambda i, *_: (0, 0)),
                pl.BlockSpec((2 * BLOCK, HALF), lambda i, *_: (0, 0)),
            ),
        ),
        compiler_params=params(8),
        name="first_dense",
    )(spot, halves, weight)


def second_dense(parts, weight):
    def body(parts_ref, weight_ref, out):
        halves = []
        for part in range(2):
            total = parts_ref[part, 0].astype(jnp.float32)
            for k in range(1, parts.shape[1]):
                total = total + parts_ref[part, k].astype(jnp.float32)
            halves.append(total.astype(jnp.bfloat16))
        value = jnp.dot(
            jnp.concatenate(halves, axis=1), weight_ref[...], preferred_element_type=jnp.float32
        )
        out[...] = value.astype(jnp.bfloat16)

    return pl.pallas_call(
        body,
        out_shape=jax.ShapeDtypeStruct((BLOCK, F), jnp.bfloat16),
        compiler_params=params(8),
        name="second_dense",
    )(parts, weight)


def gather_ring(chunk):
    ahead = [chunk]
    behind = [chunk]
    for _ in range(7):
        ahead.append(from_z(ahead[-1], 1))
        behind.append(from_z(behind[-1], -1))
    half = chunk.shape[0] // 2
    across = [from_z(ahead[7][:half], 1), from_z(behind[7][half:], -1)]
    return [*ahead, *across, *behind[:0:-1]]


def gather_quads(chunk):
    same = lax.all_gather(chunk, "zq", axis=0, tiled=True)
    above = from_z(same, 1)
    below = from_z(same, -1)
    half = same.shape[0] // 2
    across = [from_z(above[:half], 1), from_z(below[half:], -1)]
    return [same, above, *across, below]


def swap_cores(keep, send):
    other = lax.ppermute(send, "core", SWAP)
    return (keep.astype(jnp.float32) + other.astype(jnp.float32)).astype(jnp.bfloat16)


def local(
    node_feats,
    adj_vals,
    adj_col,
    adj_count,
    hist_store,
    hist_list,
    hist_adj,
    hist_row,
    hist_col,
    w_first,
    w_second,
):
    adj = adj_vals[0, 0].reshape(ROWS * SLOTS, BLOCK, BLOCK)
    cols = adj_col[0, 0].T
    counts = adj_count[0, 0]
    x_lo = lax.axis_index("x_lo")
    x_hi = lax.axis_index("x_hi")
    grid_index = lax.axis_index(GRID)
    group = jnp.where(x_lo == x_hi, (grid_index // 4) % 2, -1)
    spot = jnp.stack([x_lo, lax.axis_index("core"), group, lax.axis_index(Z)])
    spot = spot.astype(jnp.int32)
    hist_spot = jnp.stack([lax.axis_index(DOM), grid_index % 4, lax.axis_index(Z)]).astype(jnp.int32)

    payload = make_payload(
        cols,
        counts,
        pltpu.with_memory_space_constraint(node_feats, pltpu.HBM),
        pltpu.with_memory_space_constraint(hist_store, pltpu.HBM),
    )
    received = lax.all_to_all(payload, "x_lo", 0, 0, tiled=True)
    adj_held, received = lax.optimization_barrier((adj, received))
    partner = lax.ppermute(adj_held, "x_lo", SWAP)
    chunks = gather_ring(received[:, :CARRY].reshape(2 * CARRY, HALF))
    chunks = [pltpu.with_memory_space_constraint(chunk, pltpu.HBM) for chunk in chunks]
    adj = pltpu.with_memory_space_constraint(adj, pltpu.HBM)
    theirs = lax.dynamic_index_in_dim(received[:, CARRY, :80], 1 - x_lo, 0, False)
    theirs = theirs.astype(jnp.int32)
    mine = history_term(hist_list, hist_col[0], hist_row[0], hist_spot, hist_adj[0], chunks)

    tables = (cols, counts, theirs, spot)
    both = swap_cores(*tile_product(*tables, (adj, partner), chunks, ()))
    agg = add_parts(lax.all_to_all(both, SIDE, 0, 0, tiled=True))
    halves = lax.all_gather(agg, "x_lo", axis=0, tiled=False)
    hidden, chunk = first_dense(halves, w_first, spot)

    chunk, mine = lax.optimization_barrier((chunk, mine))
    extras = (mine, lax.ppermute(mine, "x_lo", SWAP))
    chunks = gather_quads(chunk)
    both = swap_cores(*tile_product(*tables, (adj, partner), chunks, extras))
    parts = lax.all_to_all(both.reshape(16, BLOCK, HALF), ALL_SIDE, 0, 0, tiled=True)
    embedding = second_dense(parts.reshape(2, 8, BLOCK, HALF), w_second)
    return hidden, embedding


def solution(mesh):
    fine = Mesh(
        mesh.devices.reshape(2, 4, 4, 2, 4, 2), ("x_lo", "zq", "zr", "x_hi", "y", "core")
    )
    placed = (
        P(DOM + GRID, None),
        P(DOM, GRID),
        P(DOM, GRID),
        P(DOM, GRID),
        P(GRID, DOM),
        P(),
        P(DOM),
        P(DOM),
        P(DOM),
        P(),
        P(),
    )
    return jax.shard_map(
        local,
        mesh=fine,
        in_specs=placed,
        out_specs=(P(DOM + GRID, None), P(DOM + GRID, None)),
        check_vma=False,
    )
```

```python
import functools

import jax
import jax.numpy as jnp
from jax import lax
from jax.experimental import pallas as pl
from jax.experimental.pallas import tpu as pltpu
from jax.sharding import Mesh, PartitionSpec as P

F = 512
HALF = 256
BLOCK = 128
HOWN = 4
ROWS = 16
SLOTS = 4
FEAT = 32
LIST = 40
WIDE = 128
META = 16
CARRY = BLOCK + 2 * FEAT
PAY = CARRY + META
DOM = ("x_lo", "zq", "zr")
Z = ("zq", "zr")
GRID = ("x_hi", "y", "core")
SIDE = ("x_hi", "y")
ALL_SIDE = ("x_lo", "x_hi", "y")
SWAP = [(0, 1), (1, 0)]


def from_z(value, offset):
    return lax.ppermute(value, Z, [((z + offset) % 16, z) for z in range(16)])


def params(mib):
    return pltpu.CompilerParams(vmem_limit_bytes=mib << 20)


def payload_body(cols, counts, feats, hist, out, feats_in, hist_in, sems):
    moves = [
        pltpu.make_async_copy(feats, feats_in, sems.at[0]),
        pltpu.make_async_copy(hist, hist_in, sems.at[1]),
    ]
    for move in moves:
        move.start()
    lane = lax.broadcasted_iota(jnp.int32, (META, HALF), 1)
    meta = jnp.zeros((META, HALF), jnp.float32)
    for row in range(ROWS):
        for slot in range(SLOTS):
            meta = jnp.where(lane == row * SLOTS + slot, cols[slot, row].astype(jnp.float32), meta)
        meta = jnp.where(lane == ROWS * SLOTS + row, counts[row].astype(jnp.float32), meta)
    meta = meta.astype(jnp.bfloat16)
    for move in moves:
        move.wait()
    for j in range(2):
        out[j, :BLOCK] = feats_in[:, j * HALF : (j + 1) * HALF]
        for k in range(2):
            start = BLOCK + k * FEAT
            out[j, start : start + FEAT] = hist_in[:, k * HALF : (k + 1) * HALF]
        out[j, CARRY:] = meta


def make_payload(cols, counts, feats, hist):
    return pl.pallas_call(
        payload_body,
        out_shape=jax.ShapeDtypeStruct((2, PAY, HALF), jnp.bfloat16),
        grid_spec=pltpu.PrefetchScalarGridSpec(
            num_scalar_prefetch=2,
            grid=(1,),
            in_specs=[pl.BlockSpec(memory_space=pltpu.HBM)] * 2,
            out_specs=pl.BlockSpec((2, PAY, HALF), lambda i, *_: (0, 0, 0)),
            scratch_shapes=[
                pltpu.VMEM(feats.shape, jnp.bfloat16),
                pltpu.VMEM(hist.shape, jnp.bfloat16),
                pltpu.SemaphoreType.DMA((2,)),
            ],
        ),
        compiler_params=params(8),
        name="payload",
    )(cols, counts, feats, hist)


def tile_body(second, stride, n_chunks, numbers, spot, *rest):
    tiles = rest[:2]
    chunks = rest[2 : 2 + n_chunks]
    if second:
        extras = rest[2 + n_chunks : 4 + n_chunks]
        keep, send, panel, adj, sems, added = rest[-6:]
    else:
        keep, send, panel, adj, sems = rest[-5:]
    core = spot[1]
    moves = []

    def move(source, target):
        moves.append(pltpu.make_async_copy(source, target, sems.at[len(moves)]))
        moves[-1].start()

    start = 0
    for source in chunks:
        move(source, panel.at[pl.ds(start, source.shape[0])])
        start += source.shape[0]
    for k in range(2):
        for c in range(4):
            move(tiles[k].at[pl.ds(16 * c, 16)], adj.at[pl.ds(64 * k + 16 * c, 16)])
    if second:
        for k in range(2):
            move(extras[k], added.at[k])

    def product(k, row):
        base = (ROWS * k + row) * SLOTS
        part = spot[0] if k == 0 else 1 - spot[0]
        count = numbers[part, ROWS * SLOTS + row]
        left = []
        right = []
        for slot in range(SLOTS):
            block = adj[base + slot]
            left.append(jnp.where(slot < count, block, jnp.zeros_like(block)))
            col = numbers[part, row * SLOTS + slot]
            z = col & 15
            ahead = z - spot[3]
            index = (ahead & 3) * 4 + (z >> 2)
            start = pl.multiple_of((index * 2 + (col >> 4)) * stride, 2 * FEAT)
            right.append(panel[pl.ds(start, BLOCK), :])
        return jnp.dot(
            jnp.concatenate(left, axis=1),
            jnp.concatenate(right, axis=0),
            preferred_element_type=jnp.float32,
        )

    def with_history(k, row, value):
        piece = added[k, row * BLOCK : (row + 1) * BLOCK, :].astype(jnp.float32)
        zero = jnp.zeros_like(piece)
        wide = [jnp.where(spot[2] == group, piece, zero) for group in range(2)]
        return value + jnp.concatenate(wide, axis=1)

    def two_rows(k, j):
        pair = [product(k, 2 * j + side) for side in range(2)]
        if second:
            pair = [with_history(k, 2 * j + side, pair[side]) for side in range(2)]
        even, odd = [value.astype(jnp.bfloat16) for value in pair]
        part = spot[0] if k == 0 else 1 - spot[0]
        where = (part, j) if second else (j, part)
        keep[where] = jnp.where(core == 0, even, odd)
        send[where] = jnp.where(core == 0, odd, even)

    for n in range(n_chunks):
        moves[n].wait()
    for k in range(2):
        for c in range(4):
            moves[n_chunks + 4 * k + c].wait()
            if second and c == 0:
                moves[n_chunks + 8 + k].wait()
            two_rows(k, 2 * c)
            two_rows(k, 2 * c + 1)


def tile_product(numbers, spot, tiles, chunks, extras):
    operands = [*tiles, *chunks, *extras]
    second = bool(extras)
    stride = sum(chunk.shape[0] for chunk in chunks) // 32
    shape = (2, ROWS // 2, BLOCK, HALF) if second else (ROWS // 2, 2, BLOCK, HALF)
    half = jax.ShapeDtypeStruct(shape, jnp.bfloat16)
    scratch = [
        pltpu.VMEM((32 * stride, HALF), jnp.bfloat16),
        pltpu.VMEM((2 * ROWS * SLOTS, BLOCK, BLOCK), jnp.bfloat16),
        pltpu.SemaphoreType.DMA((len(chunks) + 8 + len(extras),)),
    ]
    if second:
        scratch.append(pltpu.VMEM((2, ROWS * BLOCK, WIDE), jnp.bfloat16))
    out_spec = pl.BlockSpec(shape, lambda i, *_: (0,) * len(shape))
    return pl.pallas_call(
        functools.partial(tile_body, second, stride, len(chunks)),
        out_shape=(half, half),
        grid_spec=pltpu.PrefetchScalarGridSpec(
            num_scalar_prefetch=2,
            grid=(1,),
            in_specs=[pl.BlockSpec(memory_space=pltpu.HBM)] * len(operands),
            out_specs=(out_spec, out_spec),
            scratch_shapes=scratch,
        ),
        compiler_params=params(20),
        name="tile_product",
    )(numbers, spot, *operands)


def history_body(n_chunks, listed, order, rows, spot, adj, *rest):
    chunks = rest[:n_chunks]
    out, weights, store, total, sems = rest[n_chunks:]
    moves = [pltpu.make_async_copy(adj, weights, sems.at[0])]
    start = 0
    for source in chunks:
        for k in range(source.shape[0] // CARRY):
            moves.append(
                pltpu.make_async_copy(
                    source.at[pl.ds(k * CARRY + BLOCK, 2 * FEAT)],
                    store.at[pl.ds(start, 2 * FEAT)],
                    sems.at[len(moves)],
                )
            )
            start += 2 * FEAT
    for move in moves:
        move.start()
    total[...] = jnp.zeros_like(total)
    for move in moves:
        move.wait()

    def one(slot):
        block = listed[spot[0], order[slot]]
        owner = block >> 2
        piece = block & 3
        z = owner & 15
        place = (((z - spot[2]) & 3) * 4 + (z >> 2)) * 2 + (owner >> 4)
        source = pl.multiple_of(place * (2 * FEAT) + (piece >> 1) * FEAT, FEAT)
        lane = pl.multiple_of((piece & 1) * BLOCK, BLOCK)
        return lax.dot_general(
            weights[slot],
            store[pl.ds(source, FEAT), pl.ds(lane, BLOCK)],
            (((1,), (1,)), ((), ())),
            preferred_element_type=jnp.float32,
        )

    def step(n, carry):
        parts = [one(n * 5 + k) for k in range(5)]
        for k, part in enumerate(parts):
            target = pl.multiple_of(rows[n * 5 + k] * BLOCK, BLOCK)
            total[pl.ds(target, BLOCK), :FEAT] += part
        return carry

    lax.fori_loop(0, LIST // 5, step, 0)
    out[...] = pltpu.roll(total[...], spot[1] * FEAT, 1).astype(jnp.bfloat16)


def history_term(listed, order, rows, spot, adj, chunks):
    return pl.pallas_call(
        functools.partial(history_body, len(chunks)),
        out_shape=jax.ShapeDtypeStruct((ROWS * BLOCK, WIDE), jnp.bfloat16),
        grid_spec=pltpu.PrefetchScalarGridSpec(
            num_scalar_prefetch=4,
            grid=(1,),
            in_specs=[pl.BlockSpec(memory_space=pltpu.HBM)] * (1 + len(chunks)),
            out_specs=pl.BlockSpec((ROWS * BLOCK, WIDE), lambda i, *_: (0, 0)),
            scratch_shapes=[
                pltpu.VMEM(adj.shape, jnp.bfloat16),
                pltpu.VMEM((64 * FEAT, HALF), jnp.bfloat16),
                pltpu.VMEM((ROWS * BLOCK, WIDE), jnp.float32),
                pltpu.SemaphoreType.DMA((33,)),
            ],
        ),
        compiler_params=params(16),
        name="history_term",
    )(listed, order, rows, spot, adj, *chunks)


def add_parts(parts):
    def body(parts_ref, out):
        total = parts_ref[0].astype(jnp.float32)
        for k in range(1, parts.shape[0]):
            total = total + parts_ref[k].astype(jnp.float32)
        out[...] = total.astype(jnp.bfloat16)

    return pl.pallas_call(
        body,
        out_shape=jax.ShapeDtypeStruct(parts.shape[1:], jnp.bfloat16),
        compiler_params=params(8),
        name="add_parts",
    )(parts)


def first_dense(halves, weight, spot):
    def body(spot_ref, halves_ref, weight_ref, hidden, chunk):
        rows = [
            jnp.concatenate([halves_ref[0, part], halves_ref[1, part]], axis=1)
            for part in range(2)
        ]
        value = jnp.dot(
            jnp.concatenate(rows, axis=0), weight_ref[...], preferred_element_type=jnp.float32
        )
        value = jnp.maximum(value, 0.0).astype(jnp.bfloat16)
        low = spot_ref[0] == 0
        hidden[...] = jnp.where(low, value[:BLOCK], value[BLOCK:])
        chunk[...] = jnp.where(low, value[:, :HALF], value[:, HALF:])

    return pl.pallas_call(
        body,
        out_shape=(
            jax.ShapeDtypeStruct((BLOCK, F), jnp.bfloat16),
            jax.ShapeDtypeStruct((2 * BLOCK, HALF), jnp.bfloat16),
        ),
        grid_spec=pltpu.PrefetchScalarGridSpec(
            num_scalar_prefetch=1,
            grid=(1,),
            in_specs=[
                pl.BlockSpec(halves.shape, lambda i, *_: (0, 0, 0, 0)),
                pl.BlockSpec(weight.shape, lambda i, *_: (0, 0)),
            ],
            out_specs=(
                pl.BlockSpec((BLOCK, F), lambda i, *_: (0, 0)),
                pl.BlockSpec((2 * BLOCK, HALF), lambda i, *_: (0, 0)),
            ),
        ),
        compiler_params=params(8),
        name="first_dense",
    )(spot, halves, weight)


def second_dense(parts, weight):
    def body(parts_ref, weight_ref, out):
        halves = []
        for part in range(2):
            total = parts_ref[part, 0].astype(jnp.float32)
            for k in range(1, parts.shape[1]):
                total = total + parts_ref[part, k].astype(jnp.float32)
            halves.append(total.astype(jnp.bfloat16))
        value = jnp.dot(
            jnp.concatenate(halves, axis=1), weight_ref[...], preferred_element_type=jnp.float32
        )
        out[...] = value.astype(jnp.bfloat16)

    return pl.pallas_call(
        body,
        out_shape=jax.ShapeDtypeStruct((BLOCK, F), jnp.bfloat16),
        compiler_params=params(8),
        name="second_dense",
    )(parts, weight)


def gather_quads(chunk):
    same = lax.all_gather(chunk, "zq", axis=0, tiled=True)
    above = from_z(same, 1)
    below = from_z(same, -1)
    half = same.shape[0] // 2
    across = [from_z(above[:half], 1), from_z(below[half:], -1)]
    return [same, above, *across, below]


def swap_cores(keep, send):
    other = lax.ppermute(send, "core", SWAP)
    return (keep.astype(jnp.float32) + other.astype(jnp.float32)).astype(jnp.bfloat16)


def local(
    node_feats,
    adj_vals,
    adj_col,
    adj_count,
    hist_store,
    hist_list,
    hist_adj,
    hist_row,
    hist_col,
    w_first,
    w_second,
):
    adj = adj_vals[0, 0].reshape(ROWS * SLOTS, BLOCK, BLOCK)
    cols = adj_col[0, 0].T
    counts = adj_count[0, 0]
    x_lo = lax.axis_index("x_lo")
    x_hi = lax.axis_index("x_hi")
    grid_index = lax.axis_index(GRID)
    group = jnp.where(x_lo == x_hi, (grid_index // 4) % 2, -1)
    spot = jnp.stack([x_lo, lax.axis_index("core"), group, lax.axis_index(Z)])
    spot = spot.astype(jnp.int32)
    hist_spot = jnp.stack([lax.axis_index(DOM), grid_index % 4, lax.axis_index(Z)]).astype(jnp.int32)

    payload = make_payload(
        cols,
        counts,
        pltpu.with_memory_space_constraint(node_feats, pltpu.HBM),
        pltpu.with_memory_space_constraint(hist_store, pltpu.HBM),
    )
    received = lax.all_to_all(payload, "x_lo", 0, 0, tiled=True)
    adj_held, received = lax.optimization_barrier((adj, received))
    partner = lax.ppermute(adj_held, "x_lo", SWAP)
    chunks = gather_quads(received[:, :CARRY].reshape(2 * CARRY, HALF))
    chunks = [pltpu.with_memory_space_constraint(chunk, pltpu.HBM) for chunk in chunks]
    adj = pltpu.with_memory_space_constraint(adj, pltpu.HBM)
    numbers = received[:, CARRY, :80].astype(jnp.int32)
    mine = history_term(hist_list, hist_col[0], hist_row[0], hist_spot, hist_adj[0], chunks)

    tables = (numbers, spot)
    both = swap_cores(*tile_product(*tables, (adj, partner), chunks, ()))
    agg = add_parts(lax.all_to_all(both, SIDE, 0, 0, tiled=True))
    halves = lax.all_gather(agg, "x_lo", axis=0, tiled=False)
    hidden, chunk = first_dense(halves, w_first, spot)

    chunk, mine = lax.optimization_barrier((chunk, mine))
    extras = (mine, lax.ppermute(mine, "x_lo", SWAP))
    chunks = gather_quads(chunk)
    both = swap_cores(*tile_product(*tables, (adj, partner), chunks, extras))
    parts = lax.all_to_all(both.reshape(16, BLOCK, HALF), ALL_SIDE, 0, 0, tiled=True)
    embedding = second_dense(parts.reshape(2, 8, BLOCK, HALF), w_second)
    return hidden, embedding


def solution(mesh):
    fine = Mesh(
        mesh.devices.reshape(2, 4, 4, 2, 4, 2), ("x_lo", "zq", "zr", "x_hi", "y", "core")
    )
    placed = (
        P(DOM + GRID, None),
        P(DOM, GRID),
        P(DOM, GRID),
        P(DOM, GRID),
        P(GRID, DOM),
        P(),
        P(DOM),
        P(DOM),
        P(DOM),
        P(),
        P(),
    )
    return jax.shard_map(
        local,
        mesh=fine,
        in_specs=placed,
        out_specs=(P(DOM + GRID, None), P(DOM + GRID, None)),
        check_vma=False,
    )
```

```python
import functools

import jax
import jax.numpy as jnp
from jax import lax
from jax.experimental import pallas as pl
from jax.experimental.pallas import tpu as pltpu
from jax.sharding import Mesh, PartitionSpec as P

F = 512
HALF = 256
BLOCK = 128
HOWN = 4
ROWS = 16
SLOTS = 4
FEAT = 32
LIST = 40
WIDE = 128
META = 16
CARRY = BLOCK + 2 * FEAT
PAY = CARRY + META
DOM = ("x_lo", "zq", "zr")
Z = ("zq", "zr")
GRID = ("x_hi", "y", "core")
SIDE = ("x_hi", "y")
ALL_SIDE = ("x_lo", "x_hi", "y")
SWAP = [(0, 1), (1, 0)]


def from_z(value, offset):
    return lax.ppermute(value, Z, [((z + offset) % 16, z) for z in range(16)])


def params(mib):
    return pltpu.CompilerParams(vmem_limit_bytes=mib << 20)


def payload_body(cols, counts, feats, hist, out, feats_in, hist_in, sems):
    moves = [
        pltpu.make_async_copy(feats, feats_in, sems.at[0]),
        pltpu.make_async_copy(hist, hist_in, sems.at[1]),
    ]
    for move in moves:
        move.start()
    lane = lax.broadcasted_iota(jnp.int32, (META, HALF), 1)
    meta = jnp.zeros((META, HALF), jnp.float32)
    for row in range(ROWS):
        for slot in range(SLOTS):
            meta = jnp.where(lane == row * SLOTS + slot, cols[slot, row].astype(jnp.float32), meta)
        meta = jnp.where(lane == ROWS * SLOTS + row, counts[row].astype(jnp.float32), meta)
    meta = meta.astype(jnp.bfloat16)
    for move in moves:
        move.wait()
    for j in range(2):
        out[j, :BLOCK] = feats_in[:, j * HALF : (j + 1) * HALF]
        for k in range(2):
            start = BLOCK + k * FEAT
            out[j, start : start + FEAT] = hist_in[:, k * HALF : (k + 1) * HALF]
        out[j, CARRY:] = meta


def make_payload(cols, counts, feats, hist):
    return pl.pallas_call(
        payload_body,
        out_shape=jax.ShapeDtypeStruct((2, PAY, HALF), jnp.bfloat16),
        grid_spec=pltpu.PrefetchScalarGridSpec(
            num_scalar_prefetch=2,
            grid=(1,),
            in_specs=[pl.BlockSpec(memory_space=pltpu.HBM)] * 2,
            out_specs=pl.BlockSpec((2, PAY, HALF), lambda i, *_: (0, 0, 0)),
            scratch_shapes=[
                pltpu.VMEM(feats.shape, jnp.bfloat16),
                pltpu.VMEM(hist.shape, jnp.bfloat16),
                pltpu.SemaphoreType.DMA((2,)),
            ],
        ),
        compiler_params=params(8),
        name="payload",
    )(cols, counts, feats, hist)


def tile_body(second, stride, n_chunks, numbers, spot, *rest):
    tiles = rest[:2]
    chunks = rest[2 : 2 + n_chunks]
    if second:
        extras = rest[2 + n_chunks : 4 + n_chunks]
        keep, send, panel, adj, sems, added = rest[-6:]
    else:
        keep, send, panel, adj, sems = rest[-5:]
    core = spot[1]
    moves = []

    def move(source, target):
        moves.append(pltpu.make_async_copy(source, target, sems.at[len(moves)]))
        moves[-1].start()

    start = 0
    for source in chunks:
        move(source, panel.at[pl.ds(start, source.shape[0])])
        start += source.shape[0]
    for k in range(2):
        for c in range(4):
            move(tiles[k].at[pl.ds(16 * c, 16)], adj.at[pl.ds(64 * k + 16 * c, 16)])
    if second:
        for k in range(2):
            move(extras[k], added.at[k])

    def product(k, row):
        base = (ROWS * k + row) * SLOTS
        part = spot[0] if k == 0 else 1 - spot[0]
        count = numbers[part, ROWS * SLOTS + row]
        left = []
        right = []
        for slot in range(SLOTS):
            block = adj[base + slot]
            left.append(jnp.where(slot < count, block, jnp.zeros_like(block)))
            col = numbers[part, row * SLOTS + slot]
            z = col & 15
            ahead = z - spot[3]
            index = (ahead & 3) * 4 + (z >> 2)
            start = pl.multiple_of((index * 2 + (col >> 4)) * stride, 2 * FEAT)
            right.append(panel[pl.ds(start, BLOCK), :])
        return jnp.dot(
            jnp.concatenate(left, axis=1),
            jnp.concatenate(right, axis=0),
            preferred_element_type=jnp.float32,
        )

    def with_history(k, row, value):
        piece = added[k, row * BLOCK : (row + 1) * BLOCK, :].astype(jnp.float32)
        zero = jnp.zeros_like(piece)
        wide = [jnp.where(spot[2] == group, piece, zero) for group in range(2)]
        return value + jnp.concatenate(wide, axis=1)

    def two_rows(k, j):
        pair = [product(k, 2 * j + side) for side in range(2)]
        if second:
            pair = [with_history(k, 2 * j + side, pair[side]) for side in range(2)]
        even, odd = [value.astype(jnp.bfloat16) for value in pair]
        part = spot[0] if k == 0 else 1 - spot[0]
        where = (part, j) if second else (j, part)
        keep[where] = jnp.where(core == 0, even, odd)
        send[where] = jnp.where(core == 0, odd, even)

    for n in range(n_chunks):
        moves[n].wait()
    for k in range(2):
        for c in range(4):
            moves[n_chunks + 4 * k + c].wait()
            if second and c == 0:
                moves[n_chunks + 8 + k].wait()
            two_rows(k, 2 * c)
            two_rows(k, 2 * c + 1)


def tile_product(numbers, spot, tiles, chunks, extras):
    operands = [*tiles, *chunks, *extras]
    second = bool(extras)
    stride = sum(chunk.shape[0] for chunk in chunks) // 32
    shape = (2, ROWS // 2, BLOCK, HALF) if second else (ROWS // 2, 2, BLOCK, HALF)
    half = jax.ShapeDtypeStruct(shape, jnp.bfloat16)
    scratch = [
        pltpu.VMEM((32 * stride, HALF), jnp.bfloat16),
        pltpu.VMEM((2 * ROWS * SLOTS, BLOCK, BLOCK), jnp.bfloat16),
        pltpu.SemaphoreType.DMA((len(chunks) + 8 + len(extras),)),
    ]
    if second:
        scratch.append(pltpu.VMEM((2, ROWS * BLOCK, WIDE), jnp.bfloat16))
    out_spec = pl.BlockSpec(shape, lambda i, *_: (0,) * len(shape))
    return pl.pallas_call(
        functools.partial(tile_body, second, stride, len(chunks)),
        out_shape=(half, half),
        grid_spec=pltpu.PrefetchScalarGridSpec(
            num_scalar_prefetch=2,
            grid=(1,),
            in_specs=[pl.BlockSpec(memory_space=pltpu.HBM)] * len(operands),
            out_specs=(out_spec, out_spec),
            scratch_shapes=scratch,
        ),
        compiler_params=params(20),
        name="tile_product",
    )(numbers, spot, *operands)


def history_body(n_chunks, listed, order, rows, spot, adj, *rest):
    chunks = rest[:n_chunks]
    out, weights, store, total, sems = rest[n_chunks:]
    moves = [pltpu.make_async_copy(adj, weights, sems.at[0])]
    start = 0
    for source in chunks:
        for k in range(source.shape[0] // CARRY):
            moves.append(
                pltpu.make_async_copy(
                    source.at[pl.ds(k * CARRY + BLOCK, 2 * FEAT)],
                    store.at[pl.ds(start, 2 * FEAT)],
                    sems.at[len(moves)],
                )
            )
            start += 2 * FEAT
    for move in moves:
        move.start()
    total[...] = jnp.zeros_like(total)
    for move in moves:
        move.wait()

    def one(slot):
        block = listed[spot[0], order[slot]]
        owner = block >> 2
        piece = block & 3
        z = owner & 15
        place = (((z - spot[2]) & 3) * 4 + (z >> 2)) * 2 + (owner >> 4)
        source = pl.multiple_of(place * (2 * FEAT) + (piece >> 1) * FEAT, FEAT)
        lane = pl.multiple_of((piece & 1) * BLOCK, BLOCK)
        return lax.dot_general(
            weights[slot],
            store[pl.ds(source, FEAT), pl.ds(lane, BLOCK)],
            (((1,), (1,)), ((), ())),
            preferred_element_type=jnp.float32,
        )

    def step(n, carry):
        parts = [one(n * 5 + k) for k in range(5)]
        for k, part in enumerate(parts):
            target = pl.multiple_of(rows[n * 5 + k] * BLOCK, BLOCK)
            total[pl.ds(target, BLOCK), :FEAT] += part
        return carry

    lax.fori_loop(0, LIST // 5, step, 0)
    out[...] = pltpu.roll(total[...], spot[1] * FEAT, 1).astype(jnp.bfloat16)


def history_term(listed, order, rows, spot, adj, chunks):
    return pl.pallas_call(
        functools.partial(history_body, len(chunks)),
        out_shape=jax.ShapeDtypeStruct((ROWS * BLOCK, WIDE), jnp.bfloat16),
        grid_spec=pltpu.PrefetchScalarGridSpec(
            num_scalar_prefetch=4,
            grid=(1,),
            in_specs=[pl.BlockSpec(memory_space=pltpu.HBM)] * (1 + len(chunks)),
            out_specs=pl.BlockSpec((ROWS * BLOCK, WIDE), lambda i, *_: (0, 0)),
            scratch_shapes=[
                pltpu.VMEM(adj.shape, jnp.bfloat16),
                pltpu.VMEM((64 * FEAT, HALF), jnp.bfloat16),
                pltpu.VMEM((ROWS * BLOCK, WIDE), jnp.float32),
                pltpu.SemaphoreType.DMA((33,)),
            ],
        ),
        compiler_params=params(16),
        name="history_term",
    )(listed, order, rows, spot, adj, *chunks)


def add_parts(parts):
    def body(parts_ref, out):
        total = parts_ref[0].astype(jnp.float32)
        for k in range(1, parts.shape[0]):
            total = total + parts_ref[k].astype(jnp.float32)
        out[...] = total.astype(jnp.bfloat16)

    return pl.pallas_call(
        body,
        out_shape=jax.ShapeDtypeStruct(parts.shape[1:], jnp.bfloat16),
        compiler_params=params(8),
        name="add_parts",
    )(parts)


def first_dense(halves, weight, spot):
    def body(spot_ref, halves_ref, weight_ref, hidden, chunk):
        rows = [
            jnp.concatenate([halves_ref[0, part], halves_ref[1, part]], axis=1)
            for part in range(2)
        ]
        value = jnp.dot(
            jnp.concatenate(rows, axis=0), weight_ref[...], preferred_element_type=jnp.float32
        )
        value = jnp.maximum(value, 0.0).astype(jnp.bfloat16)
        low = spot_ref[0] == 0
        hidden[...] = jnp.where(low, value[:BLOCK], value[BLOCK:])
        chunk[...] = jnp.where(low, value[:, :HALF], value[:, HALF:])

    return pl.pallas_call(
        body,
        out_shape=(
            jax.ShapeDtypeStruct((BLOCK, F), jnp.bfloat16),
            jax.ShapeDtypeStruct((2 * BLOCK, HALF), jnp.bfloat16),
        ),
        grid_spec=pltpu.PrefetchScalarGridSpec(
            num_scalar_prefetch=1,
            grid=(1,),
            in_specs=[
                pl.BlockSpec(halves.shape, lambda i, *_: (0, 0, 0, 0)),
                pl.BlockSpec(weight.shape, lambda i, *_: (0, 0)),
            ],
            out_specs=(
                pl.BlockSpec((BLOCK, F), lambda i, *_: (0, 0)),
                pl.BlockSpec((2 * BLOCK, HALF), lambda i, *_: (0, 0)),
            ),
        ),
        compiler_params=params(8),
        name="first_dense",
    )(spot, halves, weight)


def second_dense(parts, weight):
    def body(parts_ref, weight_ref, out):
        halves = []
        for part in range(2):
            total = parts_ref[part, 0].astype(jnp.float32)
            for k in range(1, parts.shape[1]):
                total = total + parts_ref[part, k].astype(jnp.float32)
            halves.append(total.astype(jnp.bfloat16))
        value = jnp.dot(
            jnp.concatenate(halves, axis=1), weight_ref[...], preferred_element_type=jnp.float32
        )
        out[...] = value.astype(jnp.bfloat16)

    return pl.pallas_call(
        body,
        out_shape=jax.ShapeDtypeStruct((BLOCK, F), jnp.bfloat16),
        compiler_params=params(8),
        name="second_dense",
    )(parts, weight)


def gather_quads(chunk):
    same = lax.all_gather(chunk, "zq", axis=0, tiled=True)
    above = from_z(same, 1)
    below = from_z(same, -1)
    half = same.shape[0] // 2
    across = [from_z(above[:half], 1), from_z(below[half:], -1)]
    return [same, above, *across, below]


def swap_cores(keep, send):
    other = lax.ppermute(send, "core", SWAP)
    return (keep.astype(jnp.float32) + other.astype(jnp.float32)).astype(jnp.bfloat16)


def local(
    node_feats,
    adj_vals,
    adj_col,
    adj_count,
    hist_store,
    hist_list,
    hist_adj,
    hist_row,
    hist_col,
    w_first,
    w_second,
):
    adj = adj_vals[0, 0].reshape(ROWS * SLOTS, BLOCK, BLOCK)
    cols = pltpu.with_memory_space_constraint(adj_col[0, 0].T, pltpu.HBM)
    counts = pltpu.with_memory_space_constraint(adj_count[0, 0], pltpu.HBM)
    x_lo = lax.axis_index("x_lo")
    x_hi = lax.axis_index("x_hi")
    grid_index = lax.axis_index(GRID)
    group = jnp.where(x_lo == x_hi, (grid_index // 4) % 2, -1)
    spot = jnp.stack([x_lo, lax.axis_index("core"), group, lax.axis_index(Z)])
    spot = spot.astype(jnp.int32)
    hist_spot = jnp.stack([lax.axis_index(DOM), grid_index % 4, lax.axis_index(Z)]).astype(jnp.int32)

    payload = make_payload(
        cols,
        counts,
        pltpu.with_memory_space_constraint(node_feats, pltpu.HBM),
        pltpu.with_memory_space_constraint(hist_store, pltpu.HBM),
    )
    received = lax.all_to_all(payload, "x_lo", 0, 0, tiled=True)
    adj_held, received = lax.optimization_barrier((adj, received))
    partner = lax.ppermute(adj_held, "x_lo", SWAP)
    chunks = gather_quads(received[:, :CARRY].reshape(2 * CARRY, HALF))
    chunks = [pltpu.with_memory_space_constraint(chunk, pltpu.HBM) for chunk in chunks]
    adj = pltpu.with_memory_space_constraint(adj, pltpu.HBM)
    numbers = received[:, CARRY, :80].astype(jnp.int32)
    mine = history_term(hist_list, hist_col[0], hist_row[0], hist_spot, hist_adj[0], chunks)

    tables = (numbers, spot)
    both = swap_cores(*tile_product(*tables, (adj, partner), chunks, ()))
    agg = add_parts(lax.all_to_all(both, SIDE, 0, 0, tiled=True))
    halves = lax.all_gather(agg, "x_lo", axis=0, tiled=False)
    hidden, chunk = first_dense(
        halves, pltpu.with_memory_space_constraint(w_first, pltpu.HBM), spot
    )

    chunk, mine = lax.optimization_barrier((chunk, mine))
    extras = (mine, lax.ppermute(mine, "x_lo", SWAP))
    chunks = gather_quads(chunk)
    both = swap_cores(*tile_product(*tables, (adj, partner), chunks, extras))
    parts = lax.all_to_all(both.reshape(16, BLOCK, HALF), ALL_SIDE, 0, 0, tiled=True)
    embedding = second_dense(parts.reshape(2, 8, BLOCK, HALF), w_second)
    return hidden, embedding


def solution(mesh):
    fine = Mesh(
        mesh.devices.reshape(2, 4, 4, 2, 4, 2), ("x_lo", "zq", "zr", "x_hi", "y", "core")
    )
    placed = (
        P(DOM + GRID, None),
        P(DOM, GRID),
        P(DOM, GRID),
        P(DOM, GRID),
        P(GRID, DOM),
        P(),
        P(DOM),
        P(DOM),
        P(DOM),
        P(),
        P(),
    )
    return jax.shard_map(
        local,
        mesh=fine,
        in_specs=placed,
        out_specs=(P(DOM + GRID, None), P(DOM + GRID, None)),
        check_vma=False,
    )
```

```python
import functools

import jax
import jax.numpy as jnp
from jax import lax
from jax.experimental import pallas as pl
from jax.experimental.pallas import tpu as pltpu
from jax.sharding import Mesh, PartitionSpec as P

F = 512
HALF = 256
BLOCK = 128
HOWN = 4
ROWS = 16
SLOTS = 4
FEAT = 32
LIST = 40
WIDE = 128
META = 16
PAY = BLOCK + META
DOM = ("x_lo", "zq", "zr")
Z = ("zq", "zr")
GRID = ("x_hi", "y", "core")
SIDE = ("x_hi", "y")
ALL_SIDE = ("x_lo", "x_hi", "y")
SWAP = [(0, 1), (1, 0)]


def from_z(value, offset):
    return lax.ppermute(value, Z, [((z + offset) % 16, z) for z in range(16)])


def params(mib):
    return pltpu.CompilerParams(vmem_limit_bytes=mib << 20)


def payload_body(cols, counts, feats, hist, out, own, feats_in, hist_in, sems):
    moves = [
        pltpu.make_async_copy(feats, feats_in, sems.at[0]),
        pltpu.make_async_copy(hist, hist_in, sems.at[1]),
    ]
    for move in moves:
        move.start()
    lane = lax.broadcasted_iota(jnp.int32, (META, HALF), 1)
    meta = jnp.zeros((META, HALF), jnp.float32)
    for row in range(ROWS):
        for slot in range(SLOTS):
            meta = jnp.where(lane == row * SLOTS + slot, cols[slot, row].astype(jnp.float32), meta)
        meta = jnp.where(lane == ROWS * SLOTS + row, counts[row].astype(jnp.float32), meta)
    meta = meta.astype(jnp.bfloat16)
    for move in moves:
        move.wait()
    for j in range(2):
        out[j, :BLOCK] = feats_in[:, j * HALF : (j + 1) * HALF]
        out[j, BLOCK:] = meta
        own[j * FEAT : (j + 1) * FEAT] = hist_in[:, j * HALF : (j + 1) * HALF]


def make_payload(cols, counts, feats, hist):
    return pl.pallas_call(
        payload_body,
        out_shape=(
            jax.ShapeDtypeStruct((2, PAY, HALF), jnp.bfloat16),
            jax.ShapeDtypeStruct((2 * FEAT, HALF), jnp.bfloat16),
        ),
        grid_spec=pltpu.PrefetchScalarGridSpec(
            num_scalar_prefetch=2,
            grid=(1,),
            in_specs=[pl.BlockSpec(memory_space=pltpu.HBM)] * 2,
            out_specs=(
                pl.BlockSpec((2, PAY, HALF), lambda i, *_: (0, 0, 0)),
                pl.BlockSpec((2 * FEAT, HALF), lambda i, *_: (0, 0)),
            ),
            scratch_shapes=[
                pltpu.VMEM(feats.shape, jnp.bfloat16),
                pltpu.VMEM(hist.shape, jnp.bfloat16),
                pltpu.SemaphoreType.DMA((2,)),
            ],
        ),
        compiler_params=params(8),
        name="payload",
    )(cols, counts, feats, hist)


def tile_body(second, stride, n_chunks, numbers, spot, *rest):
    tiles = rest[:2]
    chunks = rest[2 : 2 + n_chunks]
    if second:
        extras = rest[2 + n_chunks : 4 + n_chunks]
        keep, send, panel, adj, sems, added = rest[-6:]
    else:
        keep, send, store, panel, adj, sems = rest[-6:]
    core = spot[1]
    moves = []

    def move(source, target):
        moves.append(pltpu.make_async_copy(source, target, sems.at[len(moves)]))
        moves[-1].start()

    start = 0
    for source in chunks:
        move(source, panel.at[pl.ds(start, source.shape[0])])
        start += source.shape[0]
    for k in range(2):
        for c in range(4):
            move(tiles[k].at[pl.ds(16 * c, 16)], adj.at[pl.ds(64 * k + 16 * c, 16)])
    if second:
        for k in range(2):
            move(extras[k], added.at[k])

    def product(k, row):
        base = (ROWS * k + row) * SLOTS
        part = spot[0] if k == 0 else 1 - spot[0]
        count = numbers[part, ROWS * SLOTS + row]
        left = []
        right = []
        for slot in range(SLOTS):
            block = adj[base + slot]
            left.append(jnp.where(slot < count, block, jnp.zeros_like(block)))
            col = numbers[part, row * SLOTS + slot]
            z = col & 15
            ahead = z - spot[3]
            index = (ahead & 3) * 4 + (z >> 2)
            start = pl.multiple_of(index * stride + (col >> 4) * BLOCK, 2 * FEAT)
            right.append(panel[pl.ds(start, BLOCK), :])
        return jnp.dot(
            jnp.concatenate(left, axis=1),
            jnp.concatenate(right, axis=0),
            preferred_element_type=jnp.float32,
        )

    def with_history(k, row, value):
        piece = added[k, row * BLOCK : (row + 1) * BLOCK, :].astype(jnp.float32)
        zero = jnp.zeros_like(piece)
        wide = [jnp.where(spot[2] == group, piece, zero) for group in range(2)]
        return value + jnp.concatenate(wide, axis=1)

    def two_rows(k, j):
        pair = [product(k, 2 * j + side) for side in range(2)]
        if second:
            pair = [with_history(k, 2 * j + side, pair[side]) for side in range(2)]
        even, odd = [value.astype(jnp.bfloat16) for value in pair]
        part = spot[0] if k == 0 else 1 - spot[0]
        where = (part, j) if second else (j, part)
        keep[where] = jnp.where(core == 0, even, odd)
        send[where] = jnp.where(core == 0, odd, even)

    for n in range(n_chunks):
        moves[n].wait()
    if not second:
        for d in range(16):
            source = panel.at[pl.ds(d * stride + 2 * BLOCK, 2 * FEAT)]
            move(source, store.at[pl.ds(d * 2 * FEAT, 2 * FEAT)])
    for k in range(2):
        for c in range(4):
            moves[n_chunks + 4 * k + c].wait()
            if second and c == 0:
                moves[n_chunks + 8 + k].wait()
            two_rows(k, 2 * c)
            two_rows(k, 2 * c + 1)
    if not second:
        for d in range(16):
            moves[n_chunks + 8 + d].wait()


def tile_product(numbers, spot, tiles, chunks, extras):
    operands = [*tiles, *chunks, *extras]
    second = bool(extras)
    stride = sum(chunk.shape[0] for chunk in chunks) // 16
    shape = (2, ROWS // 2, BLOCK, HALF) if second else (ROWS // 2, 2, BLOCK, HALF)
    half = jax.ShapeDtypeStruct(shape, jnp.bfloat16)
    scratch = [
        pltpu.VMEM((16 * stride, HALF), jnp.bfloat16),
        pltpu.VMEM((2 * ROWS * SLOTS, BLOCK, BLOCK), jnp.bfloat16),
        pltpu.SemaphoreType.DMA((len(chunks) + 8 + (2 if second else 16),)),
    ]
    if second:
        scratch.append(pltpu.VMEM((2, ROWS * BLOCK, WIDE), jnp.bfloat16))
    out_spec = pl.BlockSpec(shape, lambda i, *_: (0,) * len(shape))
    outs, out_specs = [half, half], [out_spec, out_spec]
    if not second:
        outs.append(jax.ShapeDtypeStruct((32 * FEAT, HALF), jnp.bfloat16))
        out_specs.append(pl.BlockSpec(memory_space=pltpu.HBM))
    return pl.pallas_call(
        functools.partial(tile_body, second, stride, len(chunks)),
        out_shape=tuple(outs),
        grid_spec=pltpu.PrefetchScalarGridSpec(
            num_scalar_prefetch=2,
            grid=(1,),
            in_specs=[pl.BlockSpec(memory_space=pltpu.HBM)] * len(operands),
            out_specs=tuple(out_specs),
            scratch_shapes=scratch,
        ),
        compiler_params=params(20),
        name="tile_product",
    )(numbers, spot, *operands)


def history_body(listed, order, rows, spot, adj, same, other, out, weights, store, total, sems):
    moves = [
        pltpu.make_async_copy(adj, weights, sems.at[0]),
        pltpu.make_async_copy(same, store.at[0], sems.at[1]),
        pltpu.make_async_copy(other, store.at[1], sems.at[2]),
    ]
    for move in moves:
        move.start()
    total[...] = jnp.zeros_like(total)
    for move in moves:
        move.wait()

    def one(slot):
        block = listed[spot[0], order[slot]]
        owner = block >> 2
        piece = block & 3
        z = owner & 15
        zone = ((z - spot[2]) & 3) * 4 + (z >> 2)
        place = zone * (2 * FEAT) + (piece >> 1) * FEAT
        source = pl.multiple_of(place, FEAT)
        lane = pl.multiple_of((piece & 1) * BLOCK, BLOCK)
        return lax.dot_general(
            weights[slot],
            store[(owner >> 4) ^ spot[3], pl.ds(source, FEAT), pl.ds(lane, BLOCK)],
            (((1,), (1,)), ((), ())),
            preferred_element_type=jnp.float32,
        )

    def step(n, carry):
        parts = [one(n * 5 + k) for k in range(5)]
        for k, part in enumerate(parts):
            target = pl.multiple_of(rows[n * 5 + k] * BLOCK, BLOCK)
            total[pl.ds(target, BLOCK), :FEAT] += part
        return carry

    lax.fori_loop(0, LIST // 5, step, 0)
    out[...] = pltpu.roll(total[...], spot[1] * FEAT, 1).astype(jnp.bfloat16)


def history_term(listed, order, rows, spot, adj, same, other):
    return pl.pallas_call(
        history_body,
        out_shape=jax.ShapeDtypeStruct((ROWS * BLOCK, WIDE), jnp.bfloat16),
        grid_spec=pltpu.PrefetchScalarGridSpec(
            num_scalar_prefetch=4,
            grid=(1,),
            in_specs=[pl.BlockSpec(memory_space=pltpu.HBM)] * 3,
            out_specs=pl.BlockSpec((ROWS * BLOCK, WIDE), lambda i, *_: (0, 0)),
            scratch_shapes=[
                pltpu.VMEM(adj.shape, jnp.bfloat16),
                pltpu.VMEM((2, *same.shape), jnp.bfloat16),
                pltpu.VMEM((ROWS * BLOCK, WIDE), jnp.float32),
                pltpu.SemaphoreType.DMA((3,)),
            ],
        ),
        compiler_params=params(16),
        name="history_term",
    )(listed, order, rows, spot, adj, same, other)


def add_parts(parts):
    def body(parts_ref, out):
        total = parts_ref[0].astype(jnp.float32)
        for k in range(1, parts.shape[0]):
            total = total + parts_ref[k].astype(jnp.float32)
        out[...] = total.astype(jnp.bfloat16)

    return pl.pallas_call(
        body,
        out_shape=jax.ShapeDtypeStruct(parts.shape[1:], jnp.bfloat16),
        compiler_params=params(8),
        name="add_parts",
    )(parts)


def first_dense(halves, weight, spot):
    def body(spot_ref, halves_ref, weight_ref, hidden, chunk):
        rows = [
            jnp.concatenate([halves_ref[0, part], halves_ref[1, part]], axis=1)
            for part in range(2)
        ]
        value = jnp.dot(
            jnp.concatenate(rows, axis=0), weight_ref[...], preferred_element_type=jnp.float32
        )
        value = jnp.maximum(value, 0.0).astype(jnp.bfloat16)
        low = spot_ref[0] == 0
        hidden[...] = jnp.where(low, value[:BLOCK], value[BLOCK:])
        chunk[...] = jnp.where(low, value[:, :HALF], value[:, HALF:])

    return pl.pallas_call(
        body,
        out_shape=(
            jax.ShapeDtypeStruct((BLOCK, F), jnp.bfloat16),
            jax.ShapeDtypeStruct((2 * BLOCK, HALF), jnp.bfloat16),
        ),
        grid_spec=pltpu.PrefetchScalarGridSpec(
            num_scalar_prefetch=1,
            grid=(1,),
            in_specs=[
                pl.BlockSpec(halves.shape, lambda i, *_: (0, 0, 0, 0)),
                pl.BlockSpec(weight.shape, lambda i, *_: (0, 0)),
            ],
            out_specs=(
                pl.BlockSpec((BLOCK, F), lambda i, *_: (0, 0)),
                pl.BlockSpec((2 * BLOCK, HALF), lambda i, *_: (0, 0)),
            ),
        ),
        compiler_params=params(8),
        name="first_dense",
    )(spot, halves, weight)


def second_dense(parts, weight):
    def body(parts_ref, weight_ref, out):
        halves = []
        for part in range(2):
            total = parts_ref[part, 0].astype(jnp.float32)
            for k in range(1, parts.shape[1]):
                total = total + parts_ref[part, k].astype(jnp.float32)
            halves.append(total.astype(jnp.bfloat16))
        value = jnp.dot(
            jnp.concatenate(halves, axis=1), weight_ref[...], preferred_element_type=jnp.float32
        )
        out[...] = value.astype(jnp.bfloat16)

    return pl.pallas_call(
        body,
        out_shape=jax.ShapeDtypeStruct((BLOCK, F), jnp.bfloat16),
        compiler_params=params(8),
        name="second_dense",
    )(parts, weight)


def gather_quads(chunk):
    same = lax.all_gather(chunk, "zq", axis=0, tiled=True)
    above = from_z(same, 1)
    below = from_z(same, -1)
    half = same.shape[0] // 2
    across = [from_z(above[:half], 1), from_z(below[half:], -1)]
    return [same, above, *across, below]


def swap_cores(keep, send):
    other = lax.ppermute(send, "core", SWAP)
    return (keep.astype(jnp.float32) + other.astype(jnp.float32)).astype(jnp.bfloat16)


def local(
    node_feats,
    adj_vals,
    adj_col,
    adj_count,
    hist_store,
    hist_list,
    hist_adj,
    hist_row,
    hist_col,
    w_first,
    w_second,
):
    adj = adj_vals[0, 0].reshape(ROWS * SLOTS, BLOCK, BLOCK)
    cols = pltpu.with_memory_space_constraint(adj_col[0, 0].T, pltpu.HBM)
    counts = pltpu.with_memory_space_constraint(adj_count[0, 0], pltpu.HBM)
    x_lo = lax.axis_index("x_lo")
    x_hi = lax.axis_index("x_hi")
    grid_index = lax.axis_index(GRID)
    group = jnp.where(x_lo == x_hi, (grid_index // 4) % 2, -1)
    spot = jnp.stack([x_lo, lax.axis_index("core"), group, lax.axis_index(Z)])
    spot = spot.astype(jnp.int32)
    hist_spot = jnp.stack([lax.axis_index(DOM), grid_index % 4, lax.axis_index(Z), x_lo]).astype(jnp.int32)

    payload, own_store = make_payload(
        cols,
        counts,
        pltpu.with_memory_space_constraint(node_feats, pltpu.HBM),
        pltpu.with_memory_space_constraint(hist_store, pltpu.HBM),
    )
    received = lax.all_to_all(payload, "x_lo", 0, 0, tiled=True)
    adj_held, received = lax.optimization_barrier((adj, received))
    partner = lax.ppermute(adj_held, "x_lo", SWAP)
    chunk = jnp.concatenate([received[0, :BLOCK], received[1, :BLOCK], own_store], axis=0)
    chunks = gather_quads(chunk)
    chunks = [pltpu.with_memory_space_constraint(chunk, pltpu.HBM) for chunk in chunks]
    adj = pltpu.with_memory_space_constraint(adj, pltpu.HBM)
    numbers = received[:, BLOCK, :80].astype(jnp.int32)
    tables = (numbers, spot)
    keep, send, store = tile_product(*tables, (adj, partner), chunks, ())
    both = swap_cores(keep, send)
    agg = add_parts(lax.all_to_all(both, SIDE, 0, 0, tiled=True))
    halves = lax.all_gather(agg, "x_lo", axis=0, tiled=False)
    hidden, chunk = first_dense(
        halves, pltpu.with_memory_space_constraint(w_first, pltpu.HBM), spot
    )

    chunk, store = lax.optimization_barrier((chunk, store))
    other_store = lax.ppermute(store, "x_lo", SWAP)
    mine = history_term(
        hist_list, hist_col[0], hist_row[0], hist_spot, hist_adj[0], store, other_store
    )
    extras = (mine, lax.ppermute(mine, "x_lo", SWAP))
    chunks = gather_quads(chunk)
    both = swap_cores(*tile_product(*tables, (adj, partner), chunks, extras))
    parts = lax.all_to_all(both.reshape(16, BLOCK, HALF), ALL_SIDE, 0, 0, tiled=True)
    embedding = second_dense(parts.reshape(2, 8, BLOCK, HALF), w_second)
    return hidden, embedding


def solution(mesh):
    fine = Mesh(
        mesh.devices.reshape(2, 4, 4, 2, 4, 2), ("x_lo", "zq", "zr", "x_hi", "y", "core")
    )
    placed = (
        P(DOM + GRID, None),
        P(DOM, GRID),
        P(DOM, GRID),
        P(DOM, GRID),
        P(GRID, DOM),
        P(),
        P(DOM),
        P(DOM),
        P(DOM),
        P(),
        P(),
    )
    return jax.shard_map(
        local,
        mesh=fine,
        in_specs=placed,
        out_specs=(P(DOM + GRID, None), P(DOM + GRID, None)),
        check_vma=False,
    )
```
